32 devices in a mesh: aper: 8 (over y, x, core), swath: 4 (over z).
Axes of the slice: x: 2, y: 2, z: 4, core: 2. Of those that a mesh axis runs over, the one named last changes fastest.
Arguments:
- polar_field: float32 [2, 1024, 4096], P(None, 'aper', 'swath'), may hold values from -6 to 6
- tap_index: int32 [3, 8, 2, 8, 128], P(None, 'aper'), may hold values from 0 to 127
- tap_weight: float32 [3, 8, 2, 8, 128], P(None, 'aper'), may hold values from -1.5 to 1.5
- range_shift: float32 [3, 8, 2, 128], P(None, 'aper'), may hold values from -8 to 8
- range_gain: float32 [3, 4096], P(None, 'swath'), may hold values from 0.1 to 1.9
- tile_owner: int32 [8, 4, 8, 1], P('aper', 'swath'), may hold values from 0 to 7; in each aligned block of 8 rows (0 to 7, 8 to 15, ..., all dimensions but the last counted through in order) at most 2 rows name the same one
- block_weights: float32 [8, 4, 8, 128, 128], P('aper', 'swath'), may hold values from -0.5 to 0.5
- kernel_index: int32 [8, 4], P('aper', 'swath'), may hold values from 0 to 15
- kernel_bank: float32 [16, 81], replicated, may hold values from -0.625 to 0.625
Outputs:
- deconvolved: float32 [2, 1024, 512], P(None, 'aper', 'swath')
The draws below stay inside these ranges and needn't reach their ends.
Inputs may be any that keep to these rules, and one draw needn't show every extreme that they name: `tile_owner`: the 8 polar blocks of one device name any one owner at most 2 times, and some device names one owner exactly 2 times; every owner is named somewhere.
All inputs are finite; a program needn't handle non-finite values.
Results may differ from the reference program's by a relative error of at most 0.00011.
Values sent between devices are 32-bit elements; how exact they have to be, the bound alone decides.
A program may use at most 128 MiB of HBM per device.

```python
import math
import jax
import jax.numpy as jnp
import numpy as np
from jax import lax

ANGLES = 128
RANGE_BINS = 1024
TAPS = 8
SECTIONS = 3
BLOCK_BINS = 128
TILE_ROWS = 128
SLOTS = 2
KERNELS = 16
N_APER = 8
N_SWATH = 4


def with_ends(values, rng, least, high):
    longest = values.shape.index(max(values.shape))
    spots = []
    for shift in (0, 1):
        where = [jax.random.randint(jax.random.fold_in(rng, axis), (), 0, length) for axis, length in enumerate(values.shape)]
        where[longest] = (where[longest] + shift) % values.shape[longest]
        spots.append(tuple(where))
    return values.at[spots[0]].set(least).at[spots[1]].set(high)


def block_levels(key, extent, shards, smallest, top_value):
    gain, own = 1.0, jax.random.fold_in(key, 6)
    for axis_at, blocks in shards:
        steps = jnp.exp(jax.random.uniform(jax.random.fold_in(own, axis_at), (blocks,), jnp.float32, smallest / len(shards), top_value / len(shards)))
        gain = gain * jnp.repeat(steps, extent[axis_at] // blocks).reshape([-1 if axis == axis_at else 1 for axis in range(len(extent))])
    return gain


def shared_out(stream_key, own, number, rows, amount, top, reach, slope):
    order = jax.random.permutation(stream_key, amount)
    crowded, ordinary = load_shares(amount, rows * top, reach, slope, True), load_shares(amount, rows * top, reach, slope, False)
    places = jnp.arange(amount)

    def named(lengths, rotation):
        used = int((lengths > 0).sum())
        fixed = max(1, used // 4)
        passed = fixed + (places - fixed + rotation * (used - fixed)) % max(1, amount - fixed)
        return jnp.zeros((amount,), jnp.int32).at[order[jnp.where(places < fixed, places, passed)]].set(jnp.asarray(lengths, jnp.int32))

    lengths = jnp.where(number % 4 == 0, named(crowded, number // 4), named(ordinary, number - number // 4 - 1))
    mixed = jax.random.permutation(jax.random.fold_in(own, 3), amount)
    source_of, taker = mixed[0:amount // 2 * 2:2], mixed[1:amount // 2 * 2:2]
    margin = jnp.minimum(lengths[source_of] - 1, reach - lengths[taker]) // 2
    margin = jnp.where((source_of == order[0]) | (taker == order[0]) | (lengths[taker] == 0), 0, jnp.maximum(margin, 0))
    passed = jax.random.randint(jax.random.fold_in(own, 4), (amount // 2,), 0, 1 << 20) % (margin + 1)
    lengths = lengths.at[source_of].add(-passed).at[taker].add(passed)
    members = jnp.searchsorted(jnp.cumsum(lengths), jnp.arange(rows * top), side="right").astype(jnp.int32)
    grid = members.reshape(top, rows).T
    grid = grid[jax.random.permutation(jax.random.fold_in(own, 1), rows)]
    rotation = jax.random.randint(jax.random.fold_in(own, 2), (rows, 1), 0, top)
    return jnp.take_along_axis(grid, (jnp.arange(top)[None, :] + rotation) % top, axis=1)


def load_shares(number_of, total, limit, slope, full):
    weights = [(1 << 20) // math.isqrt(rank ** slope) + 1 for rank in range(1, number_of + 1)]
    largest = limit if full else min(limit, max(-(-total // number_of), total * weights[0] // sum(weights)))
    least = 1 if total - largest >= number_of - 1 else 0
    given, rest = [largest] + [least] * (number_of - 1), total - largest - least * (number_of - 1)
    while rest > 0:
        candidates = [i for i in range(1, number_of) if given[i] < largest] or [i for i in range(1, number_of) if given[i] < limit]
        pool, left = sum([weights[i] for i in candidates]), rest
        for i in candidates:
            more = min(limit - given[i], max(1, left * weights[i] // pool), rest)
            given[i] = given[i] + more
            rest = rest - more
    return np.array(given)


def scatter_about(key, extent, spread, bound, split=(), held_as=jnp.bfloat16):
    drawn = jax.random.normal(key, extent, jnp.float32) * spread
    if len(split) > 0:
        drawn = block_levels(key, extent, split, -0.22, 0.18) * drawn
    return jnp.clip(drawn, min=-bound, max=bound).astype(held_as)


def setup_inputs(seed: int = 0) -> dict:
    splits = jax.random.split(jax.random.key(seed), 10)
    polar_field = scatter_about(splits[0], (2, ANGLES * N_APER, RANGE_BINS * N_SWATH), 1.0, 6.0, ((1, 8), (2, 4)), jnp.float32)
    tap_index = with_ends(jax.random.randint(splits[1], (SECTIONS, N_APER, 2, TAPS, ANGLES), 0, ANGLES), jax.random.fold_in(splits[1], 1), 0, ANGLES - 1).astype(jnp.int32)
    tap_weight = scatter_about(splits[2], (SECTIONS, N_APER, 2, TAPS, ANGLES), 0.25, 1.5, ((1, 8),), jnp.float32)
    range_shift = jnp.clip(jax.random.uniform(splits[3], (SECTIONS, N_APER, 2, ANGLES), jnp.float32, -8.0, 8.0) * block_levels(splits[3], (SECTIONS, N_APER, 2, ANGLES), ((1, 8),), -0.4, 0.0), -8.0, 8.0)
    range_gain = jnp.clip(1.0 + 0.18 * jax.random.normal(splits[4], (SECTIONS, RANGE_BINS * N_SWATH), jnp.float32), 0.1, 1.9)
    tile_owner_keys = jax.random.split(jax.random.fold_in(splits[5], 1), N_APER * N_SWATH * (RANGE_BINS // BLOCK_BINS) // (RANGE_BINS // BLOCK_BINS))
    tile_owner_turns = jax.random.permutation(jax.random.fold_in(splits[5], 3), N_APER * N_SWATH * (RANGE_BINS // BLOCK_BINS) // (RANGE_BINS // BLOCK_BINS))
    tile_owner = jax.vmap(lambda own, number: shared_out(jax.random.fold_in(splits[5], 2), own, number, RANGE_BINS // BLOCK_BINS, N_APER, 1, SLOTS, 2))(tile_owner_keys, tile_owner_turns).reshape((N_APER, N_SWATH, RANGE_BINS // BLOCK_BINS, 1))
    block_weights = scatter_about(splits[6], (N_APER, N_SWATH, RANGE_BINS // BLOCK_BINS, TILE_ROWS, ANGLES), ANGLES ** -0.5, 0.5, ((0, 8), (1, 4)), jnp.float32)
    kernel_index = with_ends(jax.random.randint(splits[7], (N_APER, N_SWATH), 0, KERNELS), jax.random.fold_in(splits[7], 1), 0, KERNELS - 1).astype(jnp.int32)
    kernel_bank = scatter_about(splits[8], (KERNELS, 81), 81 ** -0.5, 0.625, (), jnp.float32)
    return {"polar_field": polar_field, "tap_index": tap_index, "tap_weight": tap_weight, "range_shift": range_shift, "range_gain": range_gain, "tile_owner": tile_owner, "block_weights": block_weights, "kernel_index": kernel_index, "kernel_bank": kernel_bank}


HIGHEST_PRECISION = lax.Precision.HIGHEST


def transform_tables(length):
    bin_index = jnp.arange(length, dtype=jnp.int32)
    product = (bin_index[:, None] * bin_index[None, :]) % length
    phase_angle = product.astype(jnp.float32) * jnp.float32(2.0 * math.pi / length)
    return jnp.cos(phase_angle), jnp.sin(phase_angle)


def forward(signal, cos_table, sin_table):
    with_cos = jnp.dot(signal, cos_table, precision=HIGHEST_PRECISION, preferred_element_type=jnp.float32)
    with_sin = jnp.dot(signal, sin_table, precision=HIGHEST_PRECISION, preferred_element_type=jnp.float32)
    return jnp.stack([with_cos[0] + with_sin[1], with_cos[1] - with_sin[0]])


def inverse(signal, cos_table, sin_table):
    length = cos_table.shape[0]
    with_cos = jnp.dot(signal, cos_table, precision=HIGHEST_PRECISION, preferred_element_type=jnp.float32)
    with_sin = jnp.dot(signal, sin_table, precision=HIGHEST_PRECISION, preferred_element_type=jnp.float32)
    return jnp.stack([(with_cos[0] - with_sin[1]) / length, (with_cos[1] + with_sin[0]) / length])


def interp_matrix(tap_rows, weight_rows, length):
    columns = jnp.arange(length, dtype=jnp.int32)
    matches = (tap_rows[..., None] == columns).astype(jnp.float32)
    return jnp.sum(weight_rows[..., None] * matches, axis=-3)


def phase_tables(shift_rows, length):
    bin_index = jnp.arange(length, dtype=jnp.int32)
    signed = jnp.where(bin_index < length // 2, bin_index, bin_index - length).astype(jnp.float32)
    phase_angle = shift_rows[..., None] * signed * jnp.float32(-2.0 * math.pi / length)
    return jnp.cos(phase_angle), jnp.sin(phase_angle)


def steer_all(matrix, shift_rows, spectra):
    mixed = jnp.einsum("ikj,pijbr->pikbr", matrix.astype(jnp.float32), spectra.astype(jnp.float32), precision=HIGHEST_PRECISION)
    cos_phase, sin_phase = phase_tables(shift_rows, RANGE_BINS)
    cos_phase = cos_phase[:, :, None, :]
    sin_phase = sin_phase[:, :, None, :]
    return jnp.stack([cos_phase * mixed[0] - sin_phase * mixed[1], cos_phase * mixed[1] + sin_phase * mixed[0]])


def reference(polar_field, tap_index, tap_weight, range_shift, range_gain, tile_owner, block_weights, kernel_index, kernel_bank):
    cos_table, sin_table = transform_tables(RANGE_BINS)
    current = polar_field.reshape(2, N_APER, ANGLES, N_SWATH, RANGE_BINS)
    gain_rows = range_gain.reshape(SECTIONS, N_SWATH, RANGE_BINS)
    devices = np.arange(N_APER)
    for merge_step in range(SECTIONS):
        spectra = forward(current, cos_table, sin_table)
        matrices = interp_matrix(tap_index[merge_step], tap_weight[merge_step], ANGLES)
        lower_child = devices & ~(1 << merge_step)
        upper_child = devices | (1 << merge_step)
        merged = steer_all(matrices[:, 0], range_shift[merge_step][:, 0], spectra[:, lower_child])
        merged = merged + steer_all(matrices[:, 1], range_shift[merge_step][:, 1], spectra[:, upper_child])
        current = inverse(merged, cos_table, sin_table) * gain_rows[merge_step][None, None, None, :, :]
    blocks_dev = RANGE_BINS // BLOCK_BINS
    pieces = current.reshape(2, N_APER, ANGLES, N_SWATH, blocks_dev, BLOCK_BINS)
    contrib = jnp.einsum("asbxk,paksby->asbpxy", block_weights.astype(jnp.float32), pieces, precision=HIGHEST_PRECISION)
    owner_ids = tile_owner[..., 0]
    owner_hits = (owner_ids[..., None] == jnp.arange(N_APER, dtype=jnp.int32)).astype(jnp.float32)
    tile_grid = jnp.einsum("asbd,asbpxy->dspxy", owner_hits, contrib, precision=HIGHEST_PRECISION)
    cart_image = tile_grid.transpose(2, 0, 3, 1, 4).reshape(2, N_APER * TILE_ROWS, N_SWATH * BLOCK_BINS)
    padded = jnp.pad(cart_image, ((0, 0), (4, 4), (4, 4)))
    chosen = kernel_bank[kernel_index]
    result_sum = jnp.zeros((2, N_APER, TILE_ROWS, N_SWATH, BLOCK_BINS), jnp.float32)
    for offset in range(81):
        row_shift = offset // 9
        col_shift = offset % 9
        window = padded[:, row_shift:row_shift + N_APER * TILE_ROWS, col_shift:col_shift + N_SWATH * BLOCK_BINS]
        window = window.reshape(2, N_APER, TILE_ROWS, N_SWATH, BLOCK_BINS)
        result_sum = result_sum + chosen[:, :, offset][None, :, None, :, None] * window
    return result_sum.reshape(2, N_APER * TILE_ROWS, N_SWATH * BLOCK_BINS)
```

```python
import functools
import math

import jax
import jax.numpy as jnp
import numpy as np
from jax import lax
from jax.experimental import pallas as pl
from jax.experimental.pallas import tpu as pltpu
from jax.sharding import PartitionSpec as P

ANGLES = 128
RANGE_BINS = 1024
LANES = 128
GROUPS = RANGE_BINS // LANES
WIDE = 2 * LANES
TILE_ROWS = 128
TAPS = 8
MIXES = 4
BLOCK = ANGLES // MIXES
EDGE = 8
REACH = 4
MESH = pl.DeviceIdType.MESH
F32 = jnp.float32
BF16 = jnp.bfloat16


def split(value):
    high = value.astype(BF16)
    return high, (value - high.astype(F32)).astype(BF16)


def product(left, right):
    def dot(a, b):
        return jnp.dot(a, b, preferred_element_type=F32)

    return dot(left[0], right[0]) + dot(left[1], right[0]) + dot(left[0], right[1])


def turn(value):
    half = (value - jnp.floor(value + 0.5)) * F32(math.pi)
    square = half * half
    sine = F32(-1.0 / math.factorial(15))
    for order in (13, 11, 9, 7, 5, 3, 1):
        sign = 1.0 if order % 4 == 1 else -1.0
        sine = sine * square + F32(sign / math.factorial(order))
    sine = sine * half
    cosine = F32(1.0 / math.factorial(16))
    for order in (14, 12, 10, 8, 6, 4, 2, 0):
        sign = 1.0 if order % 4 == 0 else -1.0
        cosine = cosine * square + F32(sign / math.factorial(order))
    return 1.0 - 2.0 * sine * sine, 2.0 * sine * cosine


def four(x):
    (ar, ai), (br, bi), (cr, ci), (dr, di) = x
    sr, si, tr, ti = ar + cr, ai + ci, ar - cr, ai - ci
    ur, ui, vr, vi = br + dr, bi + di, br - dr, bi - di
    return [(sr + ur, si + ui), (tr + vi, ti - vr), (sr - ur, si - ui), (tr - vi, ti + vr)]


def eight(x):
    even, odd = four(x[0::2]), four(x[1::2])
    root = F32(math.sqrt(0.5))
    turned = [
        odd[0],
        ((odd[1][0] + odd[1][1]) * root, (odd[1][1] - odd[1][0]) * root),
        (odd[2][1], -odd[2][0]),
        ((odd[3][1] - odd[3][0]) * root, -(odd[3][0] + odd[3][1]) * root),
    ]
    first = [(e[0] + o[0], e[1] + o[1]) for e, o in zip(even, turned)]
    return first + [(e[0] - o[0], e[1] - o[1]) for e, o in zip(even, turned)]


def twiddle(pairs, cos_ref, sin_ref):
    out = [pairs[0]]
    for group in range(1, GROUPS):
        a, b = pairs[group]
        c, s = cos_ref[group : group + 1, :], sin_ref[group : group + 1, :]
        out.append((a * c + b * s, b * c - a * s))
    return out


def short_dft(pairs, table):
    rows = pairs[0][0].shape[0]
    stacked = jnp.concatenate([jnp.concatenate(pair, axis=1) for pair in pairs], axis=0)
    out = product(split(stacked), table)
    return [out[g * rows : (g + 1) * rows] for g in range(len(pairs))]


def forward(pairs, table, cos_ref, sin_ref):
    return short_dft(twiddle(eight(pairs), cos_ref, sin_ref), table)


def inverse(merged, table, cos_ref, sin_ref, gain):
    out = short_dft([(im, re) for re, im in merged], table)
    pairs = eight(twiddle([(o[:, :LANES], o[:, LANES:]) for o in out], cos_ref, sin_ref))
    scaled = gain * F32(1.0 / RANGE_BINS)
    result = []
    for group, (im, re) in enumerate(pairs):
        weight = scaled[:, group * LANES : (group + 1) * LANES]
        result.append((re * weight, im * weight))
    return result


def wide_product(left, right):
    def dot(a, b):
        return jnp.dot(a, b, preferred_element_type=F32)

    both = jnp.concatenate([left[0], left[1]], axis=1)
    twice = jnp.concatenate([right[0], right[0]], axis=0)
    return dot(both, twice) + dot(left[0], right[1])


def kernel(
    peers,
    swaths,
    sections,
    polar_in,
    taps,
    weights,
    shifts,
    gains,
    owner,
    weights_in,
    kernel_index,
    bank,
    table_high,
    table_low,
    cos_ref,
    sin_ref,
    result,
    polar,
    wall,
    matrix,
    phases,
    spec0,
    got0,
    total0,
    total1,
    spec1,
    spec2,
    out_high,
    out_low,
    params,
    params_got,
    owner_got,
    part,
    part_got,
    row_halo,
    col_halo,
    flipped,
    shifted,
    in_sem,
    send_sem,
    recv_sem,
    par_send,
    par_recv,
    own_send,
    own_recv,
    w_send,
    w_recv,
    part_send,
    part_recv,
    halo_send,
    halo_recv,
):
    me = lax.axis_index("aper")
    column = lax.axis_index("swath")
    levels = peers.bit_length() - 1

    row_halo[...] = jnp.zeros_like(row_halo)
    col_halo[...] = jnp.zeros_like(col_halo)

    around = [(da, ds) for da in (-1, 0, 1) for ds in (-1, 0, 1) if (da, ds) != (0, 0)]
    barrier = pltpu.get_barrier_semaphore()
    for level in range(levels):
        pl.semaphore_signal(
            barrier, inc=1, device_id=(me ^ (1 << level), column), device_id_type=MESH
        )
    for ds in (-1, 1):
        pl.semaphore_signal(
            barrier,
            inc=1,
            device_id=(me, lax.rem(column + ds + swaths, swaths)),
            device_id_type=MESH,
        )

    loads = [
        pltpu.make_async_copy(
            polar_in.at[:, pl.ds(k * BLOCK, BLOCK)],
            polar.at[:, pl.ds(k * BLOCK, BLOCK)],
            in_sem.at[k],
        )
        for k in range(MIXES)
    ]
    loads.append(pltpu.make_async_copy(weights_in.at[0, 0], wall.at[0], in_sem.at[MIXES]))
    for load in loads:
        load.start()

    bits = [lax.rem(me // (1 << step), 2) for step in range(levels)]
    table = (table_high[...], table_low[...])

    def build(index, weight):
        rows = lax.broadcasted_iota(jnp.int32, (ANGLES, ANGLES), 0).astype(F32)
        built = jnp.zeros((ANGLES, ANGLES), F32)
        for tap in range(TAPS):
            built = built + jnp.where(
                index[tap : tap + 1, :] == rows, weight[tap : tap + 1, :], F32(0.0)
            )
        return built.T

    def fill_phases(place, row):
        shift = jnp.broadcast_to(row, (ANGLES, LANES)).T
        lane = lax.broadcasted_iota(jnp.int32, (ANGLES, LANES), 1)
        signed = jnp.where(lane < LANES // 2, lane, lane - LANES).astype(F32)
        unit = shift * F32(-1.0 / RANGE_BINS)
        step_cos, step_sin = turn(unit)
        a, b = turn(unit * (signed * F32(GROUPS)))
        for group in range(GROUPS):
            phases[place, group, 0] = a
            phases[place, group, 1] = b
            if group + 1 < GROUPS:
                a, b = a * step_cos - b * step_sin, b * step_cos + a * step_sin

    def own_left(step, child):
        return build(taps[step, 0, child].astype(F32), weights[step, 0, child])

    def got_left(place):
        return build(params_got[place, :TAPS], params_got[place, TAPS : 2 * TAPS])

    def own_row(step, child):
        return shifts[step, 0, pl.ds(child, 1), :]

    def got_row(place):
        return params_got[place, 2 * TAPS : 2 * TAPS + 1]

    def steered(place, group, value):
        a = phases[place, group, 0]
        b = phases[place, group, 1]
        re, im = value[:, :LANES], value[:, LANES:]
        return jnp.concatenate([a * re - b * im, b * re + a * im], axis=1)

    def lanes(group):
        return slice(group * WIDE, (group + 1) * WIDE)

    def block(k):
        return slice(k * BLOCK, (k + 1) * BLOCK)

    def store_wide(target, rows, values):
        for group in range(GROUPS):
            target[rows, lanes(group)] = values[group]

    def merged_rows(total, rows):
        pairs = []
        for group in range(GROUPS):
            value = total[rows, lanes(group)]
            pairs.append((value[:, :LANES], value[:, LANES:]))
        return pairs

    def remote(source, target, send, recv, mask):
        return pltpu.make_async_remote_copy(
            src_ref=source,
            dst_ref=target,
            send_sem=send,
            recv_sem=recv,
            device_id=(me ^ mask, column),
            device_id_type=MESH,
        )

    for place, (step, child) in enumerate(((1, 1 - bits[1]), (2, bits[2]), (2, 1 - bits[2]))):
        params[place, :TAPS] = taps[step, 0, child].astype(F32)
        params[place, TAPS : 2 * TAPS] = weights[step, 0, child]
        params[place, 2 * TAPS : 3 * TAPS] = jnp.broadcast_to(own_row(step, child), (TAPS, LANES))

    lefts0 = [split(own_left(0, child)) for child in (bits[0], 1 - bits[0])]
    fill_phases(0, own_row(0, bits[0]))
    fill_phases(1, own_row(0, 1 - bits[0]))

    def par_copy(slot):
        source, target, mask = (
            (params.at[0], params_got.at[0], 2),
            (params.at[1], params_got.at[1], 2),
            (params.at[2], params_got.at[2], 2),
            (params.at[2], params_got.at[3], 4),
            (params_got.at[2], params_got.at[4], 4),
        )[slot]
        return remote(source, target, par_send.at[slot], par_recv.at[slot], mask)

    def own_copy(slot):
        source, target, mask = (
            (owner, owner_got.at[0], 2),
            (owner, owner_got.at[1], 4),
            (owner_got.at[0], owner_got.at[2], 4),
        )[slot]
        return remote(source, target, own_send.at[slot], own_recv.at[slot], mask)

    def w_copy(slot, q):
        mask = (2, 4, 4 if q < GROUPS // 2 else 2)[slot]
        if slot < 2:
            source = weights_in.at[0, 0, q]
        else:
            source = wall.at[1 if q < GROUPS // 2 else 2, q]
        return remote(source, wall.at[slot + 1, q], w_send.at[slot, q], w_recv.at[slot, q], mask)

    def exchange(k):
        rows = pl.ds(k * BLOCK, BLOCK)
        return remote(spec0.at[rows], got0.at[rows], send_sem.at[k], recv_sem.at[k], 1)

    for k in range(MIXES):
        rows = block(k)
        loads[k].wait()
        pairs = [
            (polar[0, rows, g * LANES : (g + 1) * LANES], polar[1, rows, g * LANES : (g + 1) * LANES])
            for g in range(GROUPS)
        ]
        store_wide(spec0, rows, forward(pairs, table, cos_ref, sin_ref))

    pl.semaphore_wait(barrier, levels + 2)
    for k in range(MIXES):
        exchange(k).start()
    for slot in range(4):
        par_copy(slot).start()
    for slot in range(2):
        own_copy(slot).start()
    order = list(range(GROUPS))
    for x_q, y_q in zip(order, order[GROUPS // 2 :] + order[: GROUPS // 2]):
        w_copy(0, x_q).start()
        w_copy(1, y_q).start()

    def mix(place, left, source, total, first):
        for group in range(GROUPS):
            value = wide_product(left, split(source[:, lanes(group)]))
            value = steered(place, group, value)
            if not first:
                value = value + total[:, lanes(group)]
            total[:, lanes(group)] = value

    def mix_two(places, left, source):
        for group in range(GROUPS):
            value = wide_product(left, split(source[:, lanes(group)]))
            for place, total, rows in zip(
                places, (total0, total1), (slice(0, ANGLES), slice(ANGLES, 2 * ANGLES))
            ):
                total[:, lanes(group)] = steered(place, group, value[rows])

    def stacked(one, two):
        return split(jnp.concatenate([one, two], axis=0))

    mix(0, lefts0[0], spec0, total0, True)
    own1 = own_left(1, bits[1])
    own2 = own_left(2, bits[2])
    fill_phases(2, own_row(1, bits[1]))
    fill_phases(4, own_row(2, bits[2]))
    for k in range(MIXES):
        exchange(k).wait()
    mix(1, lefts0[1], got0, total0, False)
    for k in range(MIXES):
        rows = block(k)
        pairs = inverse(merged_rows(total0, rows), table, cos_ref, sin_ref, gains[0:1, :])
        store_wide(spec1, rows, forward(pairs, table, cos_ref, sin_ref))

    for slot in range(3):
        par_copy(slot).wait()
    own_copy(0).wait()
    par_copy(4).start()
    own_copy(2).start()
    fill_phases(3, got_row(0))
    mix_two((2, 3), stacked(own1, got_left(0)), spec1)

    def relay(q):
        w_copy(0, q).wait()
        w_copy(2, q).start()
        w_copy(1, q + GROUPS // 2).wait()
        w_copy(2, q + GROUPS // 2).start()

    for t, total in enumerate((total0, total1)):
        for k in range(MIXES):
            rows = block(k)
            pairs = inverse(merged_rows(total, rows), table, cos_ref, sin_ref, gains[1:2, :])
            store_wide(spec2.at[t], rows, forward(pairs, table, cos_ref, sin_ref))
        if t == 0:
            relay(0)

    par_copy(3).wait()
    own_copy(1).wait()
    par_copy(4).wait()
    own_copy(2).wait()
    fill_phases(5, got_row(3))
    fill_phases(6, got_row(1))
    fill_phases(7, got_row(4))
    relay(1)

    for t in range(2):
        lefts = stacked(own2, got_left(3)) if t == 0 else stacked(got_left(1), got_left(4))
        mix_two((4 + 2 * t, 5 + 2 * t), lefts, spec2.at[t])
        if t == 0:
            relay(2)
        for slot, total in ((t, total0), (t + 2, total1)):
            for k in range(MIXES):
                rows = block(k)
                pairs = inverse(merged_rows(total, rows), table, cos_ref, sin_ref, gains[2:3, :])
                for group in range(GROUPS):
                    high, low = split(jnp.concatenate(pairs[group], axis=1))
                    out_high[slot, rows, lanes(group)] = high
                    out_low[slot, rows, lanes(group)] = low
            if t == 0 and slot == 0:
                relay(3)

    def weigh(slot, q):
        right = (out_high[slot, :, lanes(q)], out_low[slot, :, lanes(q)])
        matrix[slot, q] = wide_product(split(wall[slot, q]), right)

    def gathered(slot, d):
        first = jnp.int32(GROUPS)
        second = jnp.int32(GROUPS)
        for q in reversed(range(GROUPS)):
            name = owner[q] if slot == 0 else owner_got[slot - 1, q]
            hit = name == d
            second = jnp.where(hit, first, second)
            first = jnp.where(hit, q, first)
        value = None
        for found in (first, second):
            scale = jnp.where(found < GROUPS, F32(1.0), F32(0.0))
            term = scale * matrix[slot, jnp.minimum(found, GROUPS - 1)]
            value = term if value is None else value + term
        return value

    def part_copy(bit, half_at, slot, source, target):
        return remote(
            source, target, part_send.at[half_at, slot], part_recv.at[half_at, slot], 1 << bit
        )

    half = peers // 2

    def gather(slot, away):
        for d in range(half):
            if away:
                place, named = half + d, 2 * d + 1 - bits[0]
            else:
                place, named = d, 2 * d + bits[0]
            value = gathered(slot, named)
            part[place] = value if slot == 0 else part[place] + value

    loads[MIXES].wait()
    for q in range(GROUPS):
        weigh(0, q)
    gather(0, True)
    gather(0, False)
    for q in range(GROUPS // 2):
        w_copy(1, q).wait()
    for q in range(GROUPS):
        weigh(2, q)
    gather(2, True)
    gather(2, False)
    for q in range(GROUPS // 2, GROUPS):
        w_copy(0, q).wait()
    for q in range(GROUPS):
        weigh(1, q)
    gather(1, True)
    gather(1, False)
    for q in range(GROUPS // 2):
        w_copy(2, q).wait()
        weigh(3, q)
        w_copy(2, q + GROUPS // 2).wait()
        weigh(3, q + GROUPS // 2)
    gather(3, True)
    copies = []
    for d in range(half):
        copies.append(part_copy(0, 0, d, part.at[half + d], part_got.at[d]))
        copies[-1].start()
    gather(3, False)
    for d in range(half):
        copies[d].wait()
        part[d] = part[d] + part_got[d]
    base, here = half, 0
    count = half
    cuts = [pl.ds(h * (TILE_ROWS // 2), TILE_ROWS // 2) for h in range(2)]
    for level in range(1, levels):
        count = count // 2
        copies = []
        for e in range(count):
            for h, cut in enumerate(cuts):
                bit = level if h == 0 else levels - level
                away = 1 - bits[bit]
                index = here + (2 * e + away if h == 0 else away * count + e)
                copy = part_copy(
                    bit, h, base + e, part.at[index, cut], part_got.at[base + e, cut]
                )
                copy.start()
                copies.append(copy)
        after = peers + base - half
        for e in range(count):
            for h, cut in enumerate(cuts):
                bit = level if h == 0 else levels - level
                index = here + (2 * e + bits[bit] if h == 0 else bits[bit] * count + e)
                copies[2 * e + h].wait()
                part[after + e, cut] = part[index, cut] + part_got[base + e, cut]
        here = after
        base = base + count
    tile = part.at[here]

    for plane in range(2):
        flipped[plane] = tile[:, plane * LANES : (plane + 1) * LANES].T

    def halo_copy(da, ds):
        slot = [r for r in range(len(around)) if around[r] == (-da, -ds)][0]
        if da != 0:
            edge = 0 if da < 0 else TILE_ROWS - EDGE
            source = tile.at[pl.ds(edge, EDGE)]
            target = row_halo.at[1 if da < 0 else 0, 1 - ds]
        else:
            edge = 0 if ds < 0 else LANES - EDGE
            source = flipped.at[:, pl.ds(edge, EDGE)]
            target = col_halo.at[1 if ds < 0 else 0]
        return pltpu.make_async_remote_copy(
            src_ref=source,
            dst_ref=target,
            send_sem=halo_send.at[slot],
            recv_sem=halo_recv.at[slot],
            device_id=(me + da, column + ds),
            device_id_type=MESH,
        )

    def present(da, ds):
        found = None
        for place, step, extent in ((me, da, peers), (column, ds, swaths)):
            if step != 0:
                inside = place > 0 if step < 0 else place < extent - 1
                found = inside if found is None else jnp.logical_and(found, inside)
        return found

    for da, ds in around:

        @pl.when(present(da, ds))
        def _(da=da, ds=ds):
            halo_copy(da, ds).start()

    for da, ds in around:

        @pl.when(present(da, ds))
        def _(da=da, ds=ds):
            halo_copy(da, ds).wait_send()
            halo_copy(-da, -ds).wait_recv()

    lane = lax.broadcasted_iota(jnp.int32, (EDGE, LANES), 1)
    chosen = kernel_index[0]
    gap = jnp.zeros((LANES - 2 * EDGE, LANES), F32)
    for plane in range(2):
        cut = slice(plane * LANES, (plane + 1) * LANES)

        def strip(end):
            side = jnp.where(
                lane < LANES // 2, row_halo[end, 2, :, cut], row_halo[end, 0, :, cut]
            )
            return jnp.concatenate([row_halo[end, 1, :, cut], side], axis=1)

        side = jnp.concatenate([col_halo[1, plane], gap, col_halo[0, plane]], axis=0).T
        middle = jnp.concatenate([tile[:, cut], side], axis=1)
        whole = jnp.concatenate([strip(0), middle, strip(1)], axis=0)
        summed = jnp.zeros((TILE_ROWS, LANES), F32)
        for v in range(2 * REACH + 1):
            moved = whole if v == REACH else pltpu.roll(whole, (REACH - v) % WIDE, 1)
            shifted[v] = moved[:, :LANES]
            for u in range(2 * REACH + 1):
                start = EDGE - REACH + u
                summed = (
                    summed
                    + bank[chosen, (2 * REACH + 1) * u + v]
                    * shifted[v, start : start + TILE_ROWS, :]
                )
        result[plane] = summed


def short_tables():
    index = np.arange(LANES)
    angle = 2.0 * np.pi * (index[:, None] * index[None, :] % LANES) / LANES
    cos, sin = np.cos(angle), np.sin(angle)
    table = np.block([[cos, -sin], [sin, cos]]).astype(np.float32)
    high = table.astype(BF16)
    low = (table - high.astype(np.float32)).astype(BF16)
    spin = 2.0 * np.pi * (np.arange(GROUPS)[:, None] * index[None, :]) / RANGE_BINS
    return high, low, np.cos(spin).astype(np.float32), np.sin(spin).astype(np.float32)


def shards(peers, swaths, *args):
    (polar, taps, weights, shifts, gains, owner, block_weights, kernel_index, bank) = args
    sections = taps.shape[0]
    vmem = pl.BlockSpec(memory_space=pltpu.VMEM)
    smem = pl.BlockSpec(memory_space=pltpu.SMEM)
    anywhere = pl.BlockSpec(memory_space=pl.ANY)
    wide = pltpu.VMEM((ANGLES, GROUPS * WIDE), F32)
    tables = [jnp.asarray(t) for t in short_tables()]
    return pl.pallas_call(
        functools.partial(kernel, peers, swaths, sections),
        out_shape=jax.ShapeDtypeStruct((2, TILE_ROWS, LANES), F32),
        in_specs=[anywhere] + [vmem] * 4 + [smem, anywhere, smem, smem] + [vmem] * 4,
        out_specs=vmem,
        scratch_shapes=[
            pltpu.VMEM(polar.shape, F32),
            pltpu.VMEM((4, GROUPS, TILE_ROWS, ANGLES), F32),
            pltpu.VMEM((4, GROUPS, TILE_ROWS, WIDE), F32),
            pltpu.VMEM((8, GROUPS, 2, ANGLES, LANES), F32),
            *([wide] * 5),
            pltpu.VMEM((2, ANGLES, GROUPS * WIDE), F32),
            pltpu.VMEM((4, ANGLES, GROUPS * WIDE), BF16),
            pltpu.VMEM((4, ANGLES, GROUPS * WIDE), BF16),
            pltpu.VMEM((3, 3 * TAPS, LANES), F32),
            pltpu.VMEM((5, 3 * TAPS, LANES), F32),
            pltpu.SMEM((3, GROUPS), jnp.int32),
            pltpu.VMEM((2 * peers, TILE_ROWS, WIDE), F32),
            pltpu.VMEM((peers, TILE_ROWS, WIDE), F32),
            pltpu.VMEM((2, 3, EDGE, WIDE), F32),
            pltpu.VMEM((2, 2, EDGE, LANES), F32),
            pltpu.VMEM((2, LANES, TILE_ROWS), F32),
            pltpu.VMEM((2 * REACH + 1, TILE_ROWS + 2 * EDGE, LANES), F32),
            pltpu.SemaphoreType.DMA((MIXES + 1,)),
            pltpu.SemaphoreType.DMA((MIXES,)),
            pltpu.SemaphoreType.DMA((MIXES,)),
            pltpu.SemaphoreType.DMA((5,)),
            pltpu.SemaphoreType.DMA((5,)),
            pltpu.SemaphoreType.DMA((3,)),
            pltpu.SemaphoreType.DMA((3,)),
            pltpu.SemaphoreType.DMA((3, GROUPS)),
            pltpu.SemaphoreType.DMA((3, GROUPS)),
            pltpu.SemaphoreType.DMA((2, peers)),
            pltpu.SemaphoreType.DMA((2, peers)),
            pltpu.SemaphoreType.DMA((8,)),
            pltpu.SemaphoreType.DMA((8,)),
        ],
        compiler_params=pltpu.CompilerParams(
            collective_id=0, has_side_effects=True, vmem_limit_bytes=60 * 2**20
        ),
    )(
        polar,
        taps,
        weights,
        shifts,
        gains,
        owner.reshape(-1),
        block_weights,
        kernel_index.reshape(-1),
        bank,
        *tables,
    )


def solution(mesh):
    peers, swaths = mesh.shape["aper"], mesh.shape["swath"]
    in_specs = (
        P(None, "aper", "swath"),
        P(None, "aper", None, None, None),
        P(None, "aper", None, None, None),
        P(None, "aper", None, None),
        P(None, "swath"),
        P("aper", "swath", None, None),
        P("aper", "swath", None, None, None),
        P("aper", "swath"),
        P(),
    )
    return jax.shard_map(
        functools.partial(shards, peers, swaths),
        mesh=mesh,
        in_specs=in_specs,
        out_specs=P(None, "aper", "swath"),
        check_vma=False,
    )
```

```python
import functools
import math

import jax
import jax.numpy as jnp
import numpy as np
from jax import lax
from jax.experimental import pallas as pl
from jax.experimental.pallas import tpu as pltpu
from jax.sharding import PartitionSpec as P

ANGLES = 128
RANGE_BINS = 1024
LANES = 128
GROUPS = RANGE_BINS // LANES
WIDE = 2 * LANES
TILE_ROWS = 128
TAPS = 8
MIXES = 4
BLOCK = ANGLES // MIXES
EDGE = 8
PARTS = ((0, 64), (64, 32), (96, 32))
TALL = TILE_ROWS + 2 * EDGE
REACH = 4
MESH = pl.DeviceIdType.MESH
F32 = jnp.float32
BF16 = jnp.bfloat16


def split(value):
    high = value.astype(BF16)
    return high, (value - high.astype(F32)).astype(BF16)


def product(left, right):
    def dot(a, b):
        return jnp.dot(a, b, preferred_element_type=F32)

    return dot(left[0], right[0]) + dot(left[1], right[0]) + dot(left[0], right[1])


def turn(value):
    half = (value - jnp.floor(value + 0.5)) * F32(math.pi)
    square = half * half
    sine = F32(-1.0 / math.factorial(15))
    for order in (13, 11, 9, 7, 5, 3, 1):
        sign = 1.0 if order % 4 == 1 else -1.0
        sine = sine * square + F32(sign / math.factorial(order))
    sine = sine * half
    cosine = F32(1.0 / math.factorial(16))
    for order in (14, 12, 10, 8, 6, 4, 2, 0):
        sign = 1.0 if order % 4 == 0 else -1.0
        cosine = cosine * square + F32(sign / math.factorial(order))
    return 1.0 - 2.0 * sine * sine, 2.0 * sine * cosine


def four(x):
    (ar, ai), (br, bi), (cr, ci), (dr, di) = x
    sr, si, tr, ti = ar + cr, ai + ci, ar - cr, ai - ci
    ur, ui, vr, vi = br + dr, bi + di, br - dr, bi - di
    return [(sr + ur, si + ui), (tr + vi, ti - vr), (sr - ur, si - ui), (tr - vi, ti + vr)]


def eight(x):
    even, odd = four(x[0::2]), four(x[1::2])
    root = F32(math.sqrt(0.5))
    turned = [
        odd[0],
        ((odd[1][0] + odd[1][1]) * root, (odd[1][1] - odd[1][0]) * root),
        (odd[2][1], -odd[2][0]),
        ((odd[3][1] - odd[3][0]) * root, -(odd[3][0] + odd[3][1]) * root),
    ]
    first = [(e[0] + o[0], e[1] + o[1]) for e, o in zip(even, turned)]
    return first + [(e[0] - o[0], e[1] - o[1]) for e, o in zip(even, turned)]


def twiddle(pairs, cos_ref, sin_ref):
    out = [pairs[0]]
    for group in range(1, GROUPS):
        a, b = pairs[group]
        c, s = cos_ref[group : group + 1, :], sin_ref[group : group + 1, :]
        out.append((a * c + b * s, b * c - a * s))
    return out


def short_dft(pairs, table):
    rows = pairs[0][0].shape[0]
    stacked = jnp.concatenate([jnp.concatenate(pair, axis=1) for pair in pairs], axis=0)
    out = product(split(stacked), table)
    return [out[g * rows : (g + 1) * rows] for g in range(len(pairs))]


def forward(pairs, table, cos_ref, sin_ref):
    return short_dft(twiddle(eight(pairs), cos_ref, sin_ref), table)


def inverse(merged, table, cos_ref, sin_ref, gain):
    out = short_dft([(im, re) for re, im in merged], table)
    pairs = eight(twiddle([(o[:, :LANES], o[:, LANES:]) for o in out], cos_ref, sin_ref))
    scaled = gain * F32(1.0 / RANGE_BINS)
    result = []
    for group, (im, re) in enumerate(pairs):
        weight = scaled[:, group * LANES : (group + 1) * LANES]
        result.append((re * weight, im * weight))
    return result


def wide_product(left, right):
    def dot(a, b):
        return jnp.dot(a, b, preferred_element_type=F32)

    both = jnp.concatenate([left[0], left[1]], axis=1)
    twice = jnp.concatenate([right[0], right[0]], axis=0)
    return dot(both, twice) + dot(left[0], right[1])


def kernel(
    peers,
    swaths,
    sections,
    polar_in,
    taps,
    weights,
    shifts,
    gains,
    owner,
    weights_in,
    kernel_index,
    bank,
    table_high,
    table_low,
    cos_ref,
    sin_ref,
    result,
    polar,
    wall,
    matrix,
    phases,
    spec0,
    got0,
    total0,
    total1,
    spec1,
    spec2,
    out_high,
    out_low,
    params,
    params_got,
    owner_got,
    places,
    scales,
    away,
    kept,
    core_got,
    plane_got,
    col_halo,
    flipped,
    shifted,
    in_sem,
    send_sem,
    recv_sem,
    par_send,
    par_recv,
    own_send,
    own_recv,
    w_send,
    w_recv,
    core_send,
    core_recv,
    plane_send,
    plane_recv,
    halo_send,
    halo_recv,
):
    me = lax.axis_index("aper")
    column = lax.axis_index("swath")
    levels = peers.bit_length() - 1

    col_halo[...] = jnp.zeros_like(col_halo)

    barrier = pltpu.get_barrier_semaphore()
    for level in range(levels):
        pl.semaphore_signal(
            barrier, inc=1, device_id=(me ^ (1 << level), column), device_id_type=MESH
        )
    edges = [(column > 0, column - 1), (column < swaths - 1, column + 1)]
    for inside, place in edges:

        @pl.when(inside)
        def _(place=place):
            pl.semaphore_signal(barrier, inc=1, device_id=(me, place), device_id_type=MESH)

    greeted = levels + sum(jnp.where(inside, 1, 0) for inside, _ in edges)

    loads = [
        pltpu.make_async_copy(
            polar_in.at[:, pl.ds(k * BLOCK, BLOCK)],
            polar.at[:, pl.ds(k * BLOCK, BLOCK)],
            in_sem.at[k],
        )
        for k in range(MIXES)
    ]
    loads.append(pltpu.make_async_copy(weights_in.at[0, 0], wall.at[0], in_sem.at[MIXES]))
    for load in loads:
        load.start()

    bits = [lax.rem(me // (1 << step), 2) for step in range(levels)]
    table = (table_high[...], table_low[...])

    def build(index, weight):
        rows = lax.broadcasted_iota(jnp.int32, (ANGLES, ANGLES), 0).astype(F32)
        built = jnp.zeros((ANGLES, ANGLES), F32)
        for tap in range(TAPS):
            built = built + jnp.where(
                index[tap : tap + 1, :] == rows, weight[tap : tap + 1, :], F32(0.0)
            )
        return built.T

    def fill_phases(place, row):
        shift = jnp.broadcast_to(row, (ANGLES, LANES)).T
        lane = lax.broadcasted_iota(jnp.int32, (ANGLES, LANES), 1)
        signed = jnp.where(lane < LANES // 2, lane, lane - LANES).astype(F32)
        unit = shift * F32(-1.0 / RANGE_BINS)
        step_cos, step_sin = turn(unit)
        a, b = turn(unit * (signed * F32(GROUPS)))
        for group in range(GROUPS):
            phases[place, group, 0] = a
            phases[place, group, 1] = b
            if group + 1 < GROUPS:
                a, b = a * step_cos - b * step_sin, b * step_cos + a * step_sin

    def own_left(step, child):
        return build(taps[step, 0, child].astype(F32), weights[step, 0, child])

    def got_left(place):
        return build(params_got[place, :TAPS], params_got[place, TAPS : 2 * TAPS])

    def own_row(step, child):
        return shifts[step, 0, pl.ds(child, 1), :]

    def got_row(place):
        return params_got[place, 2 * TAPS : 2 * TAPS + 1]

    def steered(place, group, value):
        a = phases[place, group, 0]
        b = phases[place, group, 1]
        re, im = value[:, :LANES], value[:, LANES:]
        return jnp.concatenate([a * re - b * im, b * re + a * im], axis=1)

    def lanes(group):
        return slice(group * WIDE, (group + 1) * WIDE)

    def block(k):
        return slice(k * BLOCK, (k + 1) * BLOCK)

    def store_wide(target, rows, values):
        for group in range(GROUPS):
            target[rows, lanes(group)] = values[group]

    def merged_rows(total, rows):
        pairs = []
        for group in range(GROUPS):
            value = total[rows, lanes(group)]
            pairs.append((value[:, :LANES], value[:, LANES:]))
        return pairs

    def remote(source, target, send, recv, mask):
        return pltpu.make_async_remote_copy(
            src_ref=source,
            dst_ref=target,
            send_sem=send,
            recv_sem=recv,
            device_id=(me ^ mask, column),
            device_id_type=MESH,
        )

    for place, (step, child) in enumerate(((1, 1 - bits[1]), (2, bits[2]), (2, 1 - bits[2]))):
        params[place, :TAPS] = taps[step, 0, child].astype(F32)
        params[place, TAPS : 2 * TAPS] = weights[step, 0, child]
        params[place, 2 * TAPS : 3 * TAPS] = jnp.broadcast_to(own_row(step, child), (TAPS, LANES))

    lefts0 = [split(own_left(0, child)) for child in (bits[0], 1 - bits[0])]
    fill_phases(0, own_row(0, bits[0]))
    fill_phases(1, own_row(0, 1 - bits[0]))

    def par_copy(slot):
        source, target, mask = (
            (params.at[0], params_got.at[0], 2),
            (params.at[1], params_got.at[1], 2),
            (params.at[2], params_got.at[2], 2),
            (params.at[2], params_got.at[3], 4),
            (params_got.at[2], params_got.at[4], 4),
        )[slot]
        return remote(source, target, par_send.at[slot], par_recv.at[slot], mask)

    def own_copy(slot):
        source, target, mask = (
            (owner, owner_got.at[0], 2),
            (owner, owner_got.at[1], 4),
            (owner_got.at[0], owner_got.at[2], 4),
        )[slot]
        return remote(source, target, own_send.at[slot], own_recv.at[slot], mask)

    def w_copy(slot, r, h):
        mask = (2, 4, 4 if h == 0 else 2)[slot]
        start, size = PARTS[r]
        piece = (pl.ds(h * (GROUPS // 2), GROUPS // 2), pl.ds(start, size))
        source = weights_in.at[0, 0] if slot < 2 else wall.at[1 if h == 0 else 2]
        return remote(
            source.at[piece],
            wall.at[slot + 1].at[piece],
            w_send.at[slot, r, h],
            w_recv.at[slot, r, h],
            mask,
        )

    def direct(r):
        for h in range(2):
            w_copy(0, r, h).start()
            w_copy(1, r, 1 - h).start()

    def relay(r):
        for h in range(2):
            w_copy(h, r, h).wait()
            w_copy(2, r, h).start()

    def settle(r):
        w_copy(0, r, 1).wait()
        w_copy(1, r, 0).wait()
        for h in range(2):
            w_copy(2, r, h).wait()

    def exchange(k):
        rows = pl.ds(k * BLOCK, BLOCK)
        return remote(spec0.at[rows], got0.at[rows], send_sem.at[k], recv_sem.at[k], 1)

    for k in range(MIXES):
        rows = block(k)
        loads[k].wait()
        pairs = [
            (polar[0, rows, g * LANES : (g + 1) * LANES], polar[1, rows, g * LANES : (g + 1) * LANES])
            for g in range(GROUPS)
        ]
        store_wide(spec0, rows, forward(pairs, table, cos_ref, sin_ref))

    pl.semaphore_wait(barrier, greeted)
    for k in range(MIXES):
        exchange(k).start()
    for slot in range(4):
        par_copy(slot).start()
    for slot in range(2):
        own_copy(slot).start()
    direct(0)
    direct(1)

    def note_owners():
        for slot in range(4):
            for named in range(-1, peers + 1):
                first = jnp.int32(GROUPS)
                second = jnp.int32(GROUPS)
                for q in reversed(range(GROUPS)):
                    hit = (owner[q] if slot == 0 else owner_got[slot - 1, q]) == named
                    second = jnp.where(hit, first, second)
                    first = jnp.where(hit, q, first)
                for k, found in enumerate((first, second)):
                    places[slot * 2 + k, named + 1] = jnp.minimum(found, GROUPS - 1)
                    scales[slot * 2 + k, named + 1] = jnp.where(found < GROUPS, F32(1.0), F32(0.0))

    def mix(place, left, source, total, first):
        for group in range(GROUPS):
            value = wide_product(left, split(source[:, lanes(group)]))
            value = steered(place, group, value)
            if not first:
                value = value + total[:, lanes(group)]
            total[:, lanes(group)] = value

    def mix_two(places, left, source):
        for group in range(GROUPS):
            value = wide_product(left, split(source[:, lanes(group)]))
            for place, total, rows in zip(
                places, (total0, total1), (slice(0, ANGLES), slice(ANGLES, 2 * ANGLES))
            ):
                total[:, lanes(group)] = steered(place, group, value[rows])

    def stacked(one, two):
        return split(jnp.concatenate([one, two], axis=0))

    mix(0, lefts0[0], spec0, total0, True)
    own1 = own_left(1, bits[1])
    own2 = own_left(2, bits[2])
    fill_phases(2, own_row(1, bits[1]))
    fill_phases(4, own_row(2, bits[2]))
    for k in range(MIXES):
        exchange(k).wait()
    mix(1, lefts0[1], got0, total0, False)
    for k in range(MIXES):
        rows = block(k)
        pairs = inverse(merged_rows(total0, rows), table, cos_ref, sin_ref, gains[0:1, :])
        store_wide(spec1, rows, forward(pairs, table, cos_ref, sin_ref))

    for slot in range(3):
        par_copy(slot).wait()
    own_copy(0).wait()
    par_copy(4).start()
    own_copy(2).start()
    fill_phases(3, got_row(0))
    mix_two((2, 3), stacked(own1, got_left(0)), spec1)

    relay(0)

    for t, total in enumerate((total0, total1)):
        for k in range(MIXES):
            rows = block(k)
            pairs = inverse(merged_rows(total, rows), table, cos_ref, sin_ref, gains[1:2, :])
            store_wide(spec2.at[t], rows, forward(pairs, table, cos_ref, sin_ref))

    par_copy(3).wait()
    own_copy(1).wait()
    par_copy(4).wait()
    own_copy(2).wait()
    fill_phases(5, got_row(3))
    fill_phases(6, got_row(1))
    fill_phases(7, got_row(4))
    note_owners()

    for t in range(2):
        lefts = stacked(own2, got_left(3)) if t == 0 else stacked(got_left(1), got_left(4))
        mix_two((4 + 2 * t, 5 + 2 * t), lefts, spec2.at[t])
        for slot, total in ((t, total0), (t + 2, total1)):
            for k in range(MIXES):
                rows = block(k)
                pairs = inverse(merged_rows(total, rows), table, cos_ref, sin_ref, gains[2:3, :])
                for group in range(GROUPS):
                    high, low = split(jnp.concatenate(pairs[group], axis=1))
                    out_high[slot, rows, lanes(group)] = high
                    out_low[slot, rows, lanes(group)] = low
            if t == 0 and slot == 2:
                relay(1)
                direct(2)

    half = peers // 2
    mine = me // 2

    def weigh(slot, r):
        start, size = PARTS[r]
        rows = slice(start, start + size)
        for q in range(GROUPS):
            right = (out_high[slot, :, lanes(q)], out_low[slot, :, lanes(q)])
            matrix[slot, q, rows] = wide_product(split(wall[slot, q, rows]), right)

    def spans(r):
        start, size = PARTS[r]
        found = [(EDGE + start, size, 0, start)]
        if r == 0:
            found.append((0, EDGE, 1, 0))
        if r == len(PARTS) - 1:
            found.append((EDGE + TILE_ROWS, EDGE, -1, TILE_ROWS - EDGE))
        return found

    def reach(r):
        start, size = PARTS[r]
        first = 0 if r == 0 else EDGE + start
        last = TALL if r == len(PARTS) - 1 else EDGE + start + size
        return pl.ds(first, last - first)

    def gather(target, parity, r):
        for e in range(half):
            for at, size, step, start in spans(r):
                named = 2 * e + parity + step + 1
                value = None
                for slot in range(4):
                    for k in range(2):
                        spot = places[slot * 2 + k, named]
                        term = scales[slot * 2 + k, named] * matrix[slot, spot, start : start + size]
                        value = term if value is None else value + term
                target[e, at : at + size] = value

    def core_copy(r):
        return remote(
            away.at[:, reach(r)],
            core_got.at[:, reach(r)],
            core_send.at[r],
            core_recv.at[r],
            1,
        )

    def plane_copy(j, r):
        return remote(
            kept.at[mine ^ j, reach(r)],
            plane_got.at[j - 1, reach(r)],
            plane_send.at[j - 1, r],
            plane_recv.at[j - 1, r],
            2 * j,
        )

    def collect(r):
        gather(away, 1 - bits[0], r)
        core_copy(r).start()
        gather(kept, bits[0], r)

    def spread(r):
        core_copy(r).wait()
        for e in range(half):
            kept[e, reach(r)] = kept[e, reach(r)] + core_got[e, reach(r)]
        for j in range(1, half):
            plane_copy(j, r).start()

    def finish(r):
        for j in range(1, half):
            plane_copy(j, r).wait()
        value = kept[mine, reach(r)]
        for j in range(1, half):
            value = value + plane_got[j - 1, reach(r)]
        kept[mine, reach(r)] = value

    loads[MIXES].wait()
    for slot in range(4):
        if slot == 1:
            settle(0)
        weigh(slot, 0)
    collect(0)
    relay(2)
    weigh(0, 1)
    settle(1)
    for slot in range(1, 4):
        weigh(slot, 1)
    spread(0)
    collect(1)
    weigh(0, 2)
    settle(2)
    for slot in range(1, 4):
        weigh(slot, 2)
    collect(2)
    spread(1)
    spread(2)
    for r in range(len(PARTS)):
        finish(r)
    tile = kept.at[mine]

    low, high = slice(0, EDGE), slice(EDGE + TILE_ROWS, TALL)
    middle = slice(EDGE, EDGE + TILE_ROWS)
    cuts = [slice(plane * LANES, (plane + 1) * LANES) for plane in range(2)]
    for plane in range(2):
        flipped[plane] = tile[middle, cuts[plane]].T
    ends = [tile[rows, cut] for cut in cuts for rows in (low, high)]
    ends.append(jnp.zeros((LANES - 4 * EDGE, LANES), F32))
    flipped[2] = jnp.concatenate(ends, axis=0).T

    def halo_copy(side):
        edge = LANES - EDGE if side else 0
        return pltpu.make_async_remote_copy(
            src_ref=flipped.at[:, pl.ds(edge, EDGE)],
            dst_ref=col_halo.at[side],
            send_sem=halo_send.at[side],
            recv_sem=halo_recv.at[side],
            device_id=(me, column + (1 if side else -1)),
            device_id_type=MESH,
        )

    for side in range(2):

        @pl.when(edges[side][0])
        def _(side=side):
            halo_copy(side).start()

    for side in range(2):

        @pl.when(edges[side][0])
        def _(side=side):
            halo_copy(side).wait_send()
            halo_copy(1 - side).wait_recv()

    chosen = kernel_index[0]
    gap = jnp.zeros((LANES - 2 * EDGE, LANES), F32)
    sides = [
        jnp.concatenate([col_halo[0, plane], gap, col_halo[1, plane]], axis=0).T
        for plane in range(3)
    ]
    for plane in range(2):
        cut = cuts[plane]
        at = plane * 2 * EDGE
        whole = jnp.concatenate(
            [
                jnp.concatenate([tile[high, cut], sides[2][at + EDGE : at + 2 * EDGE]], axis=1),
                jnp.concatenate([tile[middle, cut], sides[plane]], axis=1),
                jnp.concatenate([tile[low, cut], sides[2][at : at + EDGE]], axis=1),
            ],
            axis=0,
        )
        summed = jnp.zeros((TILE_ROWS, LANES), F32)
        for v in range(2 * REACH + 1):
            moved = whole if v == REACH else pltpu.roll(whole, (REACH - v) % WIDE, 1)
            shifted[v] = moved[:, :LANES]
            for u in range(2 * REACH + 1):
                start = EDGE - REACH + u
                summed = (
                    summed
                    + bank[chosen, (2 * REACH + 1) * u + v]
                    * shifted[v, start : start + TILE_ROWS, :]
                )
        result[plane] = summed


def short_tables():
    index = np.arange(LANES)
    angle = 2.0 * np.pi * (index[:, None] * index[None, :] % LANES) / LANES
    cos, sin = np.cos(angle), np.sin(angle)
    table = np.block([[cos, -sin], [sin, cos]]).astype(np.float32)
    high = table.astype(BF16)
    low = (table - high.astype(np.float32)).astype(BF16)
    spin = 2.0 * np.pi * (np.arange(GROUPS)[:, None] * index[None, :]) / RANGE_BINS
    return high, low, np.cos(spin).astype(np.float32), np.sin(spin).astype(np.float32)


def shards(peers, swaths, *args):
    (polar, taps, weights, shifts, gains, owner, block_weights, kernel_index, bank) = args
    sections = taps.shape[0]
    vmem = pl.BlockSpec(memory_space=pltpu.VMEM)
    smem = pl.BlockSpec(memory_space=pltpu.SMEM)
    anywhere = pl.BlockSpec(memory_space=pl.ANY)
    wide = pltpu.VMEM((ANGLES, GROUPS * WIDE), F32)
    tables = [jnp.asarray(t) for t in short_tables()]
    return pl.pallas_call(
        functools.partial(kernel, peers, swaths, sections),
        out_shape=jax.ShapeDtypeStruct((2, TILE_ROWS, LANES), F32),
        in_specs=[anywhere] + [vmem] * 4 + [smem, anywhere, smem, smem] + [vmem] * 4,
        out_specs=vmem,
        scratch_shapes=[
            pltpu.VMEM(polar.shape, F32),
            pltpu.VMEM((4, GROUPS, TILE_ROWS, ANGLES), F32),
            pltpu.VMEM((4, GROUPS, TILE_ROWS, WIDE), F32),
            pltpu.VMEM((8, GROUPS, 2, ANGLES, LANES), F32),
            *([wide] * 5),
            pltpu.VMEM((2, ANGLES, GROUPS * WIDE), F32),
            pltpu.VMEM((4, ANGLES, GROUPS * WIDE), BF16),
            pltpu.VMEM((4, ANGLES, GROUPS * WIDE), BF16),
            pltpu.VMEM((3, 3 * TAPS, LANES), F32),
            pltpu.VMEM((5, 3 * TAPS, LANES), F32),
            pltpu.SMEM((3, GROUPS), jnp.int32),
            pltpu.SMEM((8, peers + 2), jnp.int32),
            pltpu.SMEM((8, peers + 2), F32),
            *([pltpu.VMEM((peers // 2, TALL, WIDE), F32)] * 3),
            pltpu.VMEM((peers // 2 - 1, TALL, WIDE), F32),
            pltpu.VMEM((2, 3, EDGE, LANES), F32),
            pltpu.VMEM((3, LANES, LANES), F32),
            pltpu.VMEM((2 * REACH + 1, TILE_ROWS + 2 * EDGE, LANES), F32),
            pltpu.SemaphoreType.DMA((MIXES + 1,)),
            pltpu.SemaphoreType.DMA((MIXES,)),
            pltpu.SemaphoreType.DMA((MIXES,)),
            pltpu.SemaphoreType.DMA((5,)),
            pltpu.SemaphoreType.DMA((5,)),
            pltpu.SemaphoreType.DMA((3,)),
            pltpu.SemaphoreType.DMA((3,)),
            pltpu.SemaphoreType.DMA((3, len(PARTS), 2)),
            pltpu.SemaphoreType.DMA((3, len(PARTS), 2)),
            pltpu.SemaphoreType.DMA((len(PARTS),)),
            pltpu.SemaphoreType.DMA((len(PARTS),)),
            pltpu.SemaphoreType.DMA((peers // 2 - 1, len(PARTS))),
            pltpu.SemaphoreType.DMA((peers // 2 - 1, len(PARTS))),
            pltpu.SemaphoreType.DMA((2,)),
            pltpu.SemaphoreType.DMA((2,)),
        ],
        compiler_params=pltpu.CompilerParams(
            collective_id=0, has_side_effects=True, vmem_limit_bytes=60 * 2**20
        ),
    )(
        polar,
        taps,
        weights,
        shifts,
        gains,
        owner.reshape(-1),
        block_weights,
        kernel_index.reshape(-1),
        bank,
        *tables,
    )


def solution(mesh):
    peers, swaths = mesh.shape["aper"], mesh.shape["swath"]
    in_specs = (
        P(None, "aper", "swath"),
        P(None, "aper", None, None, None),
        P(None, "aper", None, None, None),
        P(None, "aper", None, None),
        P(None, "swath"),
        P("aper", "swath", None, None),
        P("aper", "swath", None, None, None),
        P("aper", "swath"),
        P(),
    )
    return jax.shard_map(
        functools.partial(shards, peers, swaths),
        mesh=mesh,
        in_specs=in_specs,
        out_specs=P(None, "aper", "swath"),
        check_vma=False,
    )
```

```python
import functools
import math

import jax
import jax.numpy as jnp
import numpy as np
from jax import lax
from jax.experimental import pallas as pl
from jax.experimental.pallas import tpu as pltpu
from jax.sharding import PartitionSpec as P

ANGLES = 128
RANGE_BINS = 1024
LANES = 128
GROUPS = RANGE_BINS // LANES
WIDE = 2 * LANES
TILE_ROWS = 128
TAPS = 8
MIXES = 4
BLOCK = ANGLES // MIXES
EDGE = 8
PARTS = ((0, 64), (64, 32), (96, 32))
TALL = TILE_ROWS + 2 * EDGE
REACH = 4
MESH = pl.DeviceIdType.MESH
F32 = jnp.float32
BF16 = jnp.bfloat16


def split(value):
    high = value.astype(BF16)
    return high, (value - high.astype(F32)).astype(BF16)


def product(left, right):
    def dot(a, b):
        return jnp.dot(a, b, preferred_element_type=F32)

    return dot(left[0], right[0]) + dot(left[1], right[0]) + dot(left[0], right[1])


def turn(value):
    half = (value - jnp.floor(value + 0.5)) * F32(math.pi)
    square = half * half
    sine = F32(-1.0 / math.factorial(15))
    for order in (13, 11, 9, 7, 5, 3, 1):
        sign = 1.0 if order % 4 == 1 else -1.0
        sine = sine * square + F32(sign / math.factorial(order))
    sine = sine * half
    cosine = F32(1.0 / math.factorial(16))
    for order in (14, 12, 10, 8, 6, 4, 2, 0):
        sign = 1.0 if order % 4 == 0 else -1.0
        cosine = cosine * square + F32(sign / math.factorial(order))
    return 1.0 - 2.0 * sine * sine, 2.0 * sine * cosine


def four(x):
    (ar, ai), (br, bi), (cr, ci), (dr, di) = x
    sr, si, tr, ti = ar + cr, ai + ci, ar - cr, ai - ci
    ur, ui, vr, vi = br + dr, bi + di, br - dr, bi - di
    return [(sr + ur, si + ui), (tr + vi, ti - vr), (sr - ur, si - ui), (tr - vi, ti + vr)]


def eight(x):
    even, odd = four(x[0::2]), four(x[1::2])
    root = F32(math.sqrt(0.5))
    turned = [
        odd[0],
        ((odd[1][0] + odd[1][1]) * root, (odd[1][1] - odd[1][0]) * root),
        (odd[2][1], -odd[2][0]),
        ((odd[3][1] - odd[3][0]) * root, -(odd[3][0] + odd[3][1]) * root),
    ]
    first = [(e[0] + o[0], e[1] + o[1]) for e, o in zip(even, turned)]
    return first + [(e[0] - o[0], e[1] - o[1]) for e, o in zip(even, turned)]


def twiddle(pairs, cos_ref, sin_ref):
    out = [pairs[0]]
    for group in range(1, GROUPS):
        a, b = pairs[group]
        c, s = cos_ref[group : group + 1, :], sin_ref[group : group + 1, :]
        out.append((a * c + b * s, b * c - a * s))
    return out


def short_dft(pairs, table):
    rows = pairs[0][0].shape[0]
    stacked = jnp.concatenate([jnp.concatenate(pair, axis=1) for pair in pairs], axis=0)
    out = product(split(stacked), table)
    return [out[g * rows : (g + 1) * rows] for g in range(len(pairs))]


def forward(pairs, table, cos_ref, sin_ref):
    return short_dft(twiddle(eight(pairs), cos_ref, sin_ref), table)


def inverse(merged, table, cos_ref, sin_ref, gain):
    out = short_dft([(im, re) for re, im in merged], table)
    pairs = eight(twiddle([(o[:, :LANES], o[:, LANES:]) for o in out], cos_ref, sin_ref))
    scaled = gain * F32(1.0 / RANGE_BINS)
    result = []
    for group, (im, re) in enumerate(pairs):
        weight = scaled[:, group * LANES : (group + 1) * LANES]
        result.append((re * weight, im * weight))
    return result


def wide_product(left, right):
    def dot(a, b):
        return jnp.dot(a, b, preferred_element_type=F32)

    both = jnp.concatenate([left[0], left[1]], axis=1)
    twice = jnp.concatenate([right[0], right[0]], axis=0)
    return dot(both, twice) + dot(left[0], right[1])


def kernel(
    peers,
    swaths,
    sections,
    polar_in,
    taps,
    weights,
    shifts,
    gains,
    owner,
    weights_in,
    kernel_index,
    bank,
    table_high,
    table_low,
    cos_ref,
    sin_ref,
    result,
    polar,
    wall,
    matrix,
    phases,
    spec0,
    got0,
    total0,
    total1,
    spec1,
    spec2,
    out_high,
    out_low,
    params,
    params_got,
    owner_got,
    places,
    scales,
    away,
    kept,
    core_got,
    plane_got,
    owned,
    col_halo,
    flipped,
    shifted,
    in_sem,
    send_sem,
    recv_sem,
    par_send,
    par_recv,
    own_send,
    own_recv,
    w_send,
    w_recv,
    core_send,
    core_recv,
    plane_send,
    plane_recv,
    halo_send,
    halo_recv,
):
    me = lax.axis_index("aper")
    column = lax.axis_index("swath")
    levels = peers.bit_length() - 1

    col_halo[...] = jnp.zeros_like(col_halo)

    barrier = pltpu.get_barrier_semaphore()
    for level in range(levels):
        pl.semaphore_signal(
            barrier, inc=1, device_id=(me ^ (1 << level), column), device_id_type=MESH
        )
    edges = [(column > 0, column - 1), (column < swaths - 1, column + 1)]
    for inside, place in edges:

        @pl.when(inside)
        def _(place=place):
            pl.semaphore_signal(barrier, inc=1, device_id=(me, place), device_id_type=MESH)

    greeted = levels + sum(jnp.where(inside, 1, 0) for inside, _ in edges)

    loads = [
        pltpu.make_async_copy(polar_in, polar, in_sem.at[0]),
        pltpu.make_async_copy(weights_in.at[0, 0], wall.at[0], in_sem.at[1]),
    ]
    for load in loads:
        load.start()

    bits = [lax.rem(me // (1 << step), 2) for step in range(levels)]
    table = (table_high[...], table_low[...])

    def build(index, weight):
        rows = lax.broadcasted_iota(jnp.int32, (ANGLES, ANGLES), 0).astype(F32)
        built = jnp.zeros((ANGLES, ANGLES), F32)
        for tap in range(TAPS):
            built = built + jnp.where(
                index[tap : tap + 1, :] == rows, weight[tap : tap + 1, :], F32(0.0)
            )
        return built.T

    def fill_phases(place, row):
        shift = jnp.broadcast_to(row, (ANGLES, LANES)).T
        lane = lax.broadcasted_iota(jnp.int32, (ANGLES, LANES), 1)
        signed = jnp.where(lane < LANES // 2, lane, lane - LANES).astype(F32)
        unit = shift * F32(-1.0 / RANGE_BINS)
        step_cos, step_sin = turn(unit)
        a, b = turn(unit * (signed * F32(GROUPS)))
        for group in range(GROUPS):
            phases[place, group, 0] = a
            phases[place, group, 1] = b
            if group + 1 < GROUPS:
                a, b = a * step_cos - b * step_sin, b * step_cos + a * step_sin

    def own_left(step, child):
        return build(taps[step, 0, child].astype(F32), weights[step, 0, child])

    def got_left(place):
        return build(params_got[place, :TAPS], params_got[place, TAPS : 2 * TAPS])

    def own_row(step, child):
        return shifts[step, 0, pl.ds(child, 1), :]

    def got_row(place):
        return params_got[place, 2 * TAPS : 2 * TAPS + 1]

    def steered(place, group, value):
        a = phases[place, group, 0]
        b = phases[place, group, 1]
        re, im = value[:, :LANES], value[:, LANES:]
        return jnp.concatenate([a * re - b * im, b * re + a * im], axis=1)

    def lanes(group):
        return slice(group * WIDE, (group + 1) * WIDE)

    def block(k):
        return slice(k * BLOCK, (k + 1) * BLOCK)

    def store_wide(target, rows, values):
        for group in range(GROUPS):
            target[rows, lanes(group)] = values[group]

    def merged_rows(total, rows):
        pairs = []
        for group in range(GROUPS):
            value = total[rows, lanes(group)]
            pairs.append((value[:, :LANES], value[:, LANES:]))
        return pairs

    def remote(source, target, send, recv, mask):
        return pltpu.make_async_remote_copy(
            src_ref=source,
            dst_ref=target,
            send_sem=send,
            recv_sem=recv,
            device_id=(me ^ mask, column),
            device_id_type=MESH,
        )

    for place, (step, child) in enumerate(((1, 1 - bits[1]), (2, bits[2]), (2, 1 - bits[2]))):
        params[place, :TAPS] = taps[step, 0, child].astype(F32)
        params[place, TAPS : 2 * TAPS] = weights[step, 0, child]
        params[place, 2 * TAPS : 3 * TAPS] = jnp.broadcast_to(own_row(step, child), (TAPS, LANES))

    lefts0 = [split(own_left(0, child)) for child in (bits[0], 1 - bits[0])]
    fill_phases(0, own_row(0, bits[0]))
    fill_phases(1, own_row(0, 1 - bits[0]))

    def par_copy(slot):
        source, target, mask = (
            (params, params_got.at[pl.ds(0, 3)], 2),
            (params.at[2], params_got.at[3], 4),
            (params_got.at[2], params_got.at[4], 4),
        )[slot]
        return remote(source, target, par_send.at[slot], par_recv.at[slot], mask)

    def own_copy(slot):
        source, target, mask = (
            (owner, owner_got.at[0], 2),
            (owner, owner_got.at[1], 4),
            (owner_got.at[0], owner_got.at[2], 4),
        )[slot]
        return remote(source, target, own_send.at[slot], own_recv.at[slot], mask)

    def w_copy(slot, r, h):
        mask = (2, 4, 4 if h == 0 else 2)[slot]
        start, size = PARTS[r]
        piece = (pl.ds(h * (GROUPS // 2), GROUPS // 2), pl.ds(start, size))
        source = weights_in.at[0, 0] if slot < 2 else wall.at[1 if h == 0 else 2]
        return remote(
            source.at[piece],
            wall.at[slot + 1].at[piece],
            w_send.at[0],
            w_recv.at[r, h if slot == h else 2],
            mask,
        )

    def direct(r):
        for h in range(2):
            w_copy(0, r, h).start()
            w_copy(1, r, 1 - h).start()

    def relay(r):
        for h in range(2):
            w_copy(h, r, h).wait_recv()
            w_copy(2, r, h).start()

    def settle(r):
        rest = wall.at[pl.ds(1, 2), slice(None), pl.ds(*PARTS[r])]
        remote(rest, rest, w_send.at[0], w_recv.at[r, 2], 2).wait_recv()

    def sent():
        every = wall.at[pl.ds(1, 3)]
        remote(every, every, w_send.at[0], w_recv.at[0, 2], 2).wait_send()
        remote(plane_got, plane_got, plane_send.at[0], plane_recv.at[0], 2).wait_send()

    swap = remote(spec0, got0, send_sem.at[0], recv_sem.at[0], 1)

    loads[0].wait()
    for k in range(MIXES):
        rows = block(k)
        pairs = [
            (polar[0, rows, g * LANES : (g + 1) * LANES], polar[1, rows, g * LANES : (g + 1) * LANES])
            for g in range(GROUPS)
        ]
        store_wide(spec0, rows, forward(pairs, table, cos_ref, sin_ref))

    pl.semaphore_wait(barrier, greeted)
    swap.start()
    for slot in range(2):
        par_copy(slot).start()
    for slot in range(2):
        own_copy(slot).start()
    direct(0)

    def note_owners():
        for slot in range(4):
            for named in range(-1, peers + 1):
                first = jnp.int32(GROUPS)
                second = jnp.int32(GROUPS)
                for q in reversed(range(GROUPS)):
                    hit = (owner[q] if slot == 0 else owner_got[slot - 1, q]) == named
                    second = jnp.where(hit, first, second)
                    first = jnp.where(hit, q, first)
                for k, found in enumerate((first, second)):
                    places[slot * 2 + k, named + 1] = jnp.minimum(found, GROUPS - 1)
                    scales[slot * 2 + k, named + 1] = jnp.where(found < GROUPS, F32(1.0), F32(0.0))

    def mix(place, left, source, total, first):
        for group in range(GROUPS):
            value = wide_product(left, split(source[:, lanes(group)]))
            value = steered(place, group, value)
            if not first:
                value = value + total[:, lanes(group)]
            total[:, lanes(group)] = value

    def mix_two(places, left, source):
        for group in range(GROUPS):
            value = wide_product(left, split(source[:, lanes(group)]))
            for place, total, rows in zip(
                places, (total0, total1), (slice(0, ANGLES), slice(ANGLES, 2 * ANGLES))
            ):
                total[:, lanes(group)] = steered(place, group, value[rows])

    def stacked(one, two):
        return split(jnp.concatenate([one, two], axis=0))

    mix(0, lefts0[0], spec0, total0, True)
    own1 = own_left(1, bits[1])
    own2 = own_left(2, bits[2])
    fill_phases(2, own_row(1, bits[1]))
    fill_phases(4, own_row(2, bits[2]))
    swap.wait()
    par_copy(0).wait()
    own_copy(0).wait()
    par_copy(2).start()
    own_copy(2).start()
    direct(1)
    mix(1, lefts0[1], got0, total0, False)
    for k in range(MIXES):
        rows = block(k)
        pairs = inverse(merged_rows(total0, rows), table, cos_ref, sin_ref, gains[0:1, :])
        store_wide(spec1, rows, forward(pairs, table, cos_ref, sin_ref))

    fill_phases(3, got_row(0))
    mix_two((2, 3), stacked(own1, got_left(0)), spec1)

    relay(0)
    direct(2)

    for t, total in enumerate((total0, total1)):
        for k in range(MIXES):
            rows = block(k)
            pairs = inverse(merged_rows(total, rows), table, cos_ref, sin_ref, gains[1:2, :])
            store_wide(spec2.at[t], rows, forward(pairs, table, cos_ref, sin_ref))

    par_copy(1).wait()
    own_copy(1).wait()
    par_copy(2).wait()
    own_copy(2).wait()
    fill_phases(5, got_row(3))
    fill_phases(6, got_row(1))
    fill_phases(7, got_row(4))
    note_owners()

    for t in range(2):
        lefts = stacked(own2, got_left(3)) if t == 0 else stacked(got_left(1), got_left(4))
        mix_two((4 + 2 * t, 5 + 2 * t), lefts, spec2.at[t])
        for slot, total in ((t, total0), (t + 2, total1)):
            for k in range(MIXES):
                rows = block(k)
                pairs = inverse(merged_rows(total, rows), table, cos_ref, sin_ref, gains[2:3, :])
                for group in range(GROUPS):
                    high, low = split(jnp.concatenate(pairs[group], axis=1))
                    out_high[slot, rows, lanes(group)] = high
                    out_low[slot, rows, lanes(group)] = low
            if t == 0 and slot == 2:
                relay(1)

    half = peers // 2
    mine = me // 2

    def weigh(slot, r):
        start, size = PARTS[r]
        rows = slice(start, start + size)
        for q in range(GROUPS):
            right = (out_high[slot, :, lanes(q)], out_low[slot, :, lanes(q)])
            matrix[slot, q, rows] = wide_product(split(wall[slot, q, rows]), right)

    def spans(r):
        start, size = PARTS[r]
        found = [(EDGE + start, size, 0, start)]
        if r == 0:
            found.append((0, EDGE, 1, 0))
        if r == len(PARTS) - 1:
            found.append((EDGE + TILE_ROWS, EDGE, -1, TILE_ROWS - EDGE))
        return found

    def reach(r):
        start, size = PARTS[r]
        first = 0 if r == 0 else EDGE + start
        last = TALL if r == len(PARTS) - 1 else EDGE + start + size
        return pl.ds(first, last - first)

    def gather(target, parity, r):
        for e in range(half):
            for at, size, step, start in spans(r):
                named = 2 * e + parity + step + 1
                value = None
                for slot in range(4):
                    for k in range(2):
                        spot = places[slot * 2 + k, named]
                        term = scales[slot * 2 + k, named] * matrix[slot, spot, start : start + size]
                        value = term if value is None else value + term
                target[e, at : at + size] = value

    def core_copy(r):
        return remote(
            away.at[:, reach(r)],
            core_got.at[:, reach(r)],
            core_send.at[r],
            core_recv.at[r],
            1,
        )

    def plane_copy(j, r):
        return remote(
            kept.at[mine ^ j, reach(r)],
            plane_got.at[j - 1, reach(r)],
            plane_send.at[0],
            plane_recv.at[r],
            2 * j,
        )

    def collect(r):
        gather(away, 1 - bits[0], r)
        core_copy(r).start()
        gather(kept, bits[0], r)

    def spread(r):
        core_copy(r).wait()
        for e in range(half):
            kept[e, reach(r)] = kept[e, reach(r)] + core_got[e, reach(r)]
        for j in range(1, half):
            plane_copy(j, r).start()

    def finish(r):
        came = plane_got.at[:, reach(r)]
        remote(came, came, plane_send.at[0], plane_recv.at[r], 2).wait_recv()
        value = kept[mine, reach(r)]
        for j in range(1, half):
            value = value + plane_got[j - 1, reach(r)]
        owned[reach(r)] = value

    loads[1].wait()
    for slot in range(4):
        if slot == 1:
            settle(0)
        weigh(slot, 0)
    collect(0)
    relay(2)
    weigh(0, 1)
    settle(1)
    for slot in range(1, 4):
        weigh(slot, 1)
    spread(0)
    collect(1)
    weigh(0, 2)
    settle(2)
    for slot in range(1, 4):
        weigh(slot, 2)
    collect(2)
    spread(1)
    spread(2)
    for r in range(len(PARTS)):
        finish(r)
    tile = owned

    low, high = slice(0, EDGE), slice(EDGE + TILE_ROWS, TALL)
    middle = slice(EDGE, EDGE + TILE_ROWS)
    cuts = [slice(plane * LANES, (plane + 1) * LANES) for plane in range(2)]
    for plane in range(2):
        flipped[plane] = tile[middle, cuts[plane]].T
    ends = [tile[rows, cut] for cut in cuts for rows in (low, high)]
    ends.append(jnp.zeros((LANES - 4 * EDGE, LANES), F32))
    flipped[2] = jnp.concatenate(ends, axis=0).T

    def halo_copy(side):
        edge = LANES - EDGE if side else 0
        return pltpu.make_async_remote_copy(
            src_ref=flipped.at[:, pl.ds(edge, EDGE)],
            dst_ref=col_halo.at[side],
            send_sem=halo_send.at[side],
            recv_sem=halo_recv.at[side],
            device_id=(me, column + (1 if side else -1)),
            device_id_type=MESH,
        )

    for side in range(2):

        @pl.when(edges[side][0])
        def _(side=side):
            halo_copy(side).start()

    sent()
    for side in range(2):

        @pl.when(edges[side][0])
        def _(side=side):
            halo_copy(side).wait_send()
            halo_copy(1 - side).wait_recv()

    chosen = kernel_index[0]
    gap = jnp.zeros((LANES - 2 * EDGE, LANES), F32)
    sides = [
        jnp.concatenate([col_halo[0, plane], gap, col_halo[1, plane]], axis=0).T
        for plane in range(3)
    ]
    for plane in range(2):
        cut = cuts[plane]
        at = plane * 2 * EDGE
        whole = jnp.concatenate(
            [
                jnp.concatenate([tile[high, cut], sides[2][at + EDGE : at + 2 * EDGE]], axis=1),
                jnp.concatenate([tile[middle, cut], sides[plane]], axis=1),
                jnp.concatenate([tile[low, cut], sides[2][at : at + EDGE]], axis=1),
            ],
            axis=0,
        )
        summed = jnp.zeros((TILE_ROWS, LANES), F32)
        for v in range(2 * REACH + 1):
            moved = whole if v == REACH else pltpu.roll(whole, (REACH - v) % WIDE, 1)
            shifted[v] = moved[:, :LANES]
            for u in range(2 * REACH + 1):
                start = EDGE - REACH + u
                summed = (
                    summed
                    + bank[chosen, (2 * REACH + 1) * u + v]
                    * shifted[v, start : start + TILE_ROWS, :]
                )
        result[plane] = summed


def short_tables():
    index = np.arange(LANES)
    angle = 2.0 * np.pi * (index[:, None] * index[None, :] % LANES) / LANES
    cos, sin = np.cos(angle), np.sin(angle)
    table = np.block([[cos, -sin], [sin, cos]]).astype(np.float32)
    high = table.astype(BF16)
    low = (table - high.astype(np.float32)).astype(BF16)
    spin = 2.0 * np.pi * (np.arange(GROUPS)[:, None] * index[None, :]) / RANGE_BINS
    return high, low, np.cos(spin).astype(np.float32), np.sin(spin).astype(np.float32)


def shards(peers, swaths, *args):
    (polar, taps, weights, shifts, gains, owner, block_weights, kernel_index, bank) = args
    sections = taps.shape[0]
    vmem = pl.BlockSpec(memory_space=pltpu.VMEM)
    smem = pl.BlockSpec(memory_space=pltpu.SMEM)
    anywhere = pl.BlockSpec(memory_space=pl.ANY)
    wide = pltpu.VMEM((ANGLES, GROUPS * WIDE), F32)
    tables = [jnp.asarray(t) for t in short_tables()]
    return pl.pallas_call(
        functools.partial(kernel, peers, swaths, sections),
        out_shape=jax.ShapeDtypeStruct((2, TILE_ROWS, LANES), F32),
        in_specs=[anywhere] + [vmem] * 4 + [smem, anywhere, smem, smem] + [vmem] * 4,
        out_specs=vmem,
        scratch_shapes=[
            pltpu.VMEM(polar.shape, F32),
            pltpu.VMEM((4, GROUPS, TILE_ROWS, ANGLES), F32),
            pltpu.VMEM((4, GROUPS, TILE_ROWS, WIDE), F32),
            pltpu.VMEM((8, GROUPS, 2, ANGLES, LANES), F32),
            *([wide] * 5),
            pltpu.VMEM((2, ANGLES, GROUPS * WIDE), F32),
            pltpu.VMEM((4, ANGLES, GROUPS * WIDE), BF16),
            pltpu.VMEM((4, ANGLES, GROUPS * WIDE), BF16),
            pltpu.VMEM((3, 3 * TAPS, LANES), F32),
            pltpu.VMEM((5, 3 * TAPS, LANES), F32),
            pltpu.SMEM((3, GROUPS), jnp.int32),
            pltpu.SMEM((8, peers + 2), jnp.int32),
            pltpu.SMEM((8, peers + 2), F32),
            *([pltpu.VMEM((peers // 2, TALL, WIDE), F32)] * 3),
            pltpu.VMEM((peers // 2 - 1, TALL, WIDE), F32),
            pltpu.VMEM((TALL, WIDE), F32),
            pltpu.VMEM((2, 3, EDGE, LANES), F32),
            pltpu.VMEM((3, LANES, LANES), F32),
            pltpu.VMEM((2 * REACH + 1, TILE_ROWS + 2 * EDGE, LANES), F32),
            pltpu.SemaphoreType.DMA((2,)),
            pltpu.SemaphoreType.DMA((1,)),
            pltpu.SemaphoreType.DMA((1,)),
            pltpu.SemaphoreType.DMA((3,)),
            pltpu.SemaphoreType.DMA((3,)),
            pltpu.SemaphoreType.DMA((3,)),
            pltpu.SemaphoreType.DMA((3,)),
            pltpu.SemaphoreType.DMA((1,)),
            pltpu.SemaphoreType.DMA((len(PARTS), 3)),
            pltpu.SemaphoreType.DMA((len(PARTS),)),
            pltpu.SemaphoreType.DMA((len(PARTS),)),
            pltpu.SemaphoreType.DMA((1,)),
            pltpu.SemaphoreType.DMA((len(PARTS),)),
            pltpu.SemaphoreType.DMA((2,)),
            pltpu.SemaphoreType.DMA((2,)),
        ],
        compiler_params=pltpu.CompilerParams(
            collective_id=0, has_side_effects=True, vmem_limit_bytes=60 * 2**20
        ),
    )(
        polar,
        taps,
        weights,
        shifts,
        gains,
        owner.reshape(-1),
        block_weights,
        kernel_index.reshape(-1),
        bank,
        *tables,
    )


def solution(mesh):
    peers, swaths = mesh.shape["aper"], mesh.shape["swath"]
    in_specs = (
        P(None, "aper", "swath"),
        P(None, "aper", None, None, None),
        P(None, "aper", None, None, None),
        P(None, "aper", None, None),
        P(None, "swath"),
        P("aper", "swath", None, None),
        P("aper", "swath", None, None, None),
        P("aper", "swath"),
        P(),
    )
    return jax.shard_map(
        functools.partial(shards, peers, swaths),
        mesh=mesh,
        in_specs=in_specs,
        out_specs=P(None, "aper", "swath"),
        check_vma=False,
    )
```

```python
import functools
import math

import jax
import jax.numpy as jnp
import numpy as np
from jax import lax
from jax.experimental import pallas as pl
from jax.experimental.pallas import tpu as pltpu
from jax.sharding import PartitionSpec as P

ANGLES = 128
RANGE_BINS = 1024
LANES = 128
GROUPS = RANGE_BINS // LANES
WIDE = 2 * LANES
TILE_ROWS = 128
TAPS = 8
MIXES = 4
BLOCK = ANGLES // MIXES
EDGE = 8
PARTS = ((0, 64), (64, 32), (96, 32))
TALL = TILE_ROWS + 2 * EDGE
REACH = 4
MESH = pl.DeviceIdType.MESH
F32 = jnp.float32
BF16 = jnp.bfloat16


def split(value):
    high = value.astype(BF16)
    return high, (value - high.astype(F32)).astype(BF16)


def product(left, right):
    def dot(a, b):
        return jnp.dot(a, b, preferred_element_type=F32)

    return dot(left[0], right[0]) + dot(left[1], right[0]) + dot(left[0], right[1])


def turn(value):
    half = (value - jnp.floor(value + 0.5)) * F32(math.pi)
    square = half * half
    sine = F32(-1.0 / math.factorial(15))
    for order in (13, 11, 9, 7, 5, 3, 1):
        sign = 1.0 if order % 4 == 1 else -1.0
        sine = sine * square + F32(sign / math.factorial(order))
    sine = sine * half
    cosine = F32(1.0 / math.factorial(16))
    for order in (14, 12, 10, 8, 6, 4, 2, 0):
        sign = 1.0 if order % 4 == 0 else -1.0
        cosine = cosine * square + F32(sign / math.factorial(order))
    return 1.0 - 2.0 * sine * sine, 2.0 * sine * cosine


def four(x):
    (ar, ai), (br, bi), (cr, ci), (dr, di) = x
    sr, si, tr, ti = ar + cr, ai + ci, ar - cr, ai - ci
    ur, ui, vr, vi = br + dr, bi + di, br - dr, bi - di
    return [(sr + ur, si + ui), (tr + vi, ti - vr), (sr - ur, si - ui), (tr - vi, ti + vr)]


def eight(x):
    even, odd = four(x[0::2]), four(x[1::2])
    root = F32(math.sqrt(0.5))
    turned = [
        odd[0],
        ((odd[1][0] + odd[1][1]) * root, (odd[1][1] - odd[1][0]) * root),
        (odd[2][1], -odd[2][0]),
        ((odd[3][1] - odd[3][0]) * root, -(odd[3][0] + odd[3][1]) * root),
    ]
    first = [(e[0] + o[0], e[1] + o[1]) for e, o in zip(even, turned)]
    return first + [(e[0] - o[0], e[1] - o[1]) for e, o in zip(even, turned)]


def twiddle(pairs, cos_ref, sin_ref):
    out = [pairs[0]]
    for group in range(1, GROUPS):
        a, b = pairs[group]
        c, s = cos_ref[group : group + 1, :], sin_ref[group : group + 1, :]
        out.append((a * c + b * s, b * c - a * s))
    return out


def short_dft(pairs, table):
    rows = pairs[0][0].shape[0]
    stacked = jnp.concatenate([jnp.concatenate(pair, axis=1) for pair in pairs], axis=0)
    out = product(split(stacked), table)
    return [out[g * rows : (g + 1) * rows] for g in range(len(pairs))]


def forward(pairs, table, cos_ref, sin_ref):
    return short_dft(twiddle(eight(pairs), cos_ref, sin_ref), table)


def inverse(merged, table, cos_ref, sin_ref, gain):
    out = short_dft([(im, re) for re, im in merged], table)
    pairs = eight(twiddle([(o[:, :LANES], o[:, LANES:]) for o in out], cos_ref, sin_ref))
    scaled = gain * F32(1.0 / RANGE_BINS)
    result = []
    for group, (im, re) in enumerate(pairs):
        weight = scaled[:, group * LANES : (group + 1) * LANES]
        result.append((re * weight, im * weight))
    return result


def wide_product(left, right):
    def dot(a, b):
        return jnp.dot(a, b, preferred_element_type=F32)

    both = jnp.concatenate([left[0], left[1]], axis=1)
    twice = jnp.concatenate([right[0], right[0]], axis=0)
    return dot(both, twice) + dot(left[0], right[1])


def kernel(
    peers,
    swaths,
    sections,
    polar_in,
    taps,
    weights,
    shifts,
    gains,
    owner,
    weights_in,
    kernel_index,
    bank,
    table_high,
    table_low,
    cos_ref,
    sin_ref,
    result,
    polar,
    wall,
    matrix,
    phases,
    spec0,
    got0,
    total0,
    total1,
    spec1,
    spec2,
    out_high,
    out_low,
    params,
    params_got,
    owner_got,
    places,
    scales,
    away,
    kept,
    core_got,
    plane_got,
    owned,
    col_halo,
    flipped,
    shifted,
    inside,
    in_sem,
    send_sem,
    recv_sem,
    par_send,
    par_recv,
    own_send,
    own_recv,
    w_send,
    w_recv,
    core_send,
    core_recv,
    plane_send,
    plane_recv,
    halo_send,
    halo_recv,
):
    me = lax.axis_index("aper")
    column = lax.axis_index("swath")
    levels = peers.bit_length() - 1

    col_halo[...] = jnp.zeros_like(col_halo)

    barrier = pltpu.get_barrier_semaphore()
    for level in range(levels):
        pl.semaphore_signal(
            barrier, inc=1, device_id=(me ^ (1 << level), column), device_id_type=MESH
        )
    edges = [(column > 0, column - 1), (column < swaths - 1, column + 1)]
    for within, place in edges:

        @pl.when(within)
        def _(place=place):
            pl.semaphore_signal(barrier, inc=1, device_id=(me, place), device_id_type=MESH)

    greeted = levels + sum(jnp.where(within, 1, 0) for within, _ in edges)

    loads = [
        pltpu.make_async_copy(polar_in, polar, in_sem.at[0]),
        pltpu.make_async_copy(weights_in.at[0, 0], wall.at[0], in_sem.at[1]),
    ]
    for load in loads:
        load.start()

    bits = [lax.rem(me // (1 << step), 2) for step in range(levels)]
    table = (table_high[...], table_low[...])

    def build(index, weight):
        rows = lax.broadcasted_iota(jnp.int32, (ANGLES, ANGLES), 0).astype(F32)
        built = jnp.zeros((ANGLES, ANGLES), F32)
        for tap in range(TAPS):
            built = built + jnp.where(
                index[tap : tap + 1, :] == rows, weight[tap : tap + 1, :], F32(0.0)
            )
        return built.T

    def fill_phases(place, row):
        shift = jnp.broadcast_to(row, (ANGLES, LANES)).T
        lane = lax.broadcasted_iota(jnp.int32, (ANGLES, LANES), 1)
        signed = jnp.where(lane < LANES // 2, lane, lane - LANES).astype(F32)
        unit = shift * F32(-1.0 / RANGE_BINS)
        step_cos, step_sin = turn(unit)
        a, b = turn(unit * (signed * F32(GROUPS)))
        for group in range(GROUPS):
            phases[place, group, 0] = a
            phases[place, group, 1] = b
            if group + 1 < GROUPS:
                a, b = a * step_cos - b * step_sin, b * step_cos + a * step_sin

    def own_left(step, child):
        return build(taps[step, 0, child].astype(F32), weights[step, 0, child])

    def got_left(place):
        return build(params_got[place, :TAPS], params_got[place, TAPS : 2 * TAPS])

    def own_row(step, child):
        return shifts[step, 0, pl.ds(child, 1), :]

    def got_row(place):
        return params_got[place, 2 * TAPS : 2 * TAPS + 1]

    def steered(place, group, value):
        a = phases[place, group, 0]
        b = phases[place, group, 1]
        re, im = value[:, :LANES], value[:, LANES:]
        return jnp.concatenate([a * re - b * im, b * re + a * im], axis=1)

    def lanes(group):
        return slice(group * WIDE, (group + 1) * WIDE)

    def block(k):
        return slice(k * BLOCK, (k + 1) * BLOCK)

    def store_wide(target, rows, values):
        for group in range(GROUPS):
            target[rows, lanes(group)] = values[group]

    def merged_rows(total, rows):
        pairs = []
        for group in range(GROUPS):
            value = total[rows, lanes(group)]
            pairs.append((value[:, :LANES], value[:, LANES:]))
        return pairs

    def remote(source, target, send, recv, mask):
        return pltpu.make_async_remote_copy(
            src_ref=source,
            dst_ref=target,
            send_sem=send,
            recv_sem=recv,
            device_id=(me ^ mask, column),
            device_id_type=MESH,
        )

    for place, (step, child) in enumerate(((1, 1 - bits[1]), (2, bits[2]), (2, 1 - bits[2]))):
        params[place, :TAPS] = taps[step, 0, child].astype(F32)
        params[place, TAPS : 2 * TAPS] = weights[step, 0, child]
        params[place, 2 * TAPS : 3 * TAPS] = jnp.broadcast_to(own_row(step, child), (TAPS, LANES))

    lefts0 = [split(own_left(0, child)) for child in (bits[0], 1 - bits[0])]
    fill_phases(0, own_row(0, bits[0]))
    fill_phases(1, own_row(0, 1 - bits[0]))

    def par_copy(slot):
        source, target, mask = (
            (params, params_got.at[pl.ds(0, 3)], 2),
            (params.at[2], params_got.at[3], 4),
            (params_got.at[2], params_got.at[4], 4),
        )[slot]
        return remote(source, target, par_send.at[slot], par_recv.at[slot], mask)

    def own_copy(slot):
        source, target, mask = (
            (owner, owner_got.at[0], 2),
            (owner, owner_got.at[1], 4),
            (owner_got.at[0], owner_got.at[2], 4),
        )[slot]
        return remote(source, target, own_send.at[slot], own_recv.at[slot], mask)

    def w_copy(slot, r, h):
        mask = (2, 4, 4 if h == 0 else 2)[slot]
        start, size = PARTS[r]
        piece = (pl.ds(h * (GROUPS // 2), GROUPS // 2), pl.ds(start, size))
        source = weights_in.at[0, 0] if slot < 2 else wall.at[1 if h == 0 else 2]
        return remote(
            source.at[piece],
            wall.at[slot + 1].at[piece],
            w_send.at[0],
            w_recv.at[r, h if slot == h else 2],
            mask,
        )

    def direct(r):
        for h in range(2):
            w_copy(0, r, h).start()
            w_copy(1, r, 1 - h).start()

    def relay(r):
        for h in range(2):
            w_copy(h, r, h).wait_recv()
            w_copy(2, r, h).start()

    def settle(r):
        rest = wall.at[pl.ds(1, 2), slice(None), pl.ds(*PARTS[r])]
        remote(rest, rest, w_send.at[0], w_recv.at[r, 2], 2).wait_recv()

    def sent():
        every = wall.at[pl.ds(1, 3)]
        remote(every, every, w_send.at[0], w_recv.at[0, 2], 2).wait_send()
        remote(plane_got, plane_got, plane_send.at[0], plane_recv.at[0], 2).wait_send()

    swap = remote(spec0, got0, send_sem.at[0], recv_sem.at[0], 1)

    loads[0].wait()
    for k in range(MIXES):
        rows = block(k)
        pairs = [
            (polar[0, rows, g * LANES : (g + 1) * LANES], polar[1, rows, g * LANES : (g + 1) * LANES])
            for g in range(GROUPS)
        ]
        store_wide(spec0, rows, forward(pairs, table, cos_ref, sin_ref))

    pl.semaphore_wait(barrier, greeted)
    swap.start()
    for slot in range(2):
        par_copy(slot).start()
    for slot in range(2):
        own_copy(slot).start()
    direct(0)

    def note_owners():
        for slot in range(4):
            for named in range(-1, peers + 1):
                first = jnp.int32(GROUPS)
                second = jnp.int32(GROUPS)
                for q in reversed(range(GROUPS)):
                    hit = (owner[q] if slot == 0 else owner_got[slot - 1, q]) == named
                    second = jnp.where(hit, first, second)
                    first = jnp.where(hit, q, first)
                for k, found in enumerate((first, second)):
                    places[slot * 2 + k, named + 1] = jnp.minimum(found, GROUPS - 1)
                    scales[slot * 2 + k, named + 1] = jnp.where(found < GROUPS, F32(1.0), F32(0.0))

    def mix(place, left, source, total, first):
        for group in range(GROUPS):
            value = wide_product(left, split(source[:, lanes(group)]))
            value = steered(place, group, value)
            if not first:
                value = value + total[:, lanes(group)]
            total[:, lanes(group)] = value

    def mix_two(places, left, source):
        for group in range(GROUPS):
            value = wide_product(left, split(source[:, lanes(group)]))
            for place, total, rows in zip(
                places, (total0, total1), (slice(0, ANGLES), slice(ANGLES, 2 * ANGLES))
            ):
                total[:, lanes(group)] = steered(place, group, value[rows])

    def stacked(one, two):
        return split(jnp.concatenate([one, two], axis=0))

    mix(0, lefts0[0], spec0, total0, True)
    own1 = own_left(1, bits[1])
    own2 = own_left(2, bits[2])
    fill_phases(2, own_row(1, bits[1]))
    fill_phases(4, own_row(2, bits[2]))
    swap.wait()
    par_copy(0).wait()
    own_copy(0).wait()
    par_copy(2).start()
    own_copy(2).start()
    direct(1)
    mix(1, lefts0[1], got0, total0, False)
    for k in range(MIXES):
        rows = block(k)
        pairs = inverse(merged_rows(total0, rows), table, cos_ref, sin_ref, gains[0:1, :])
        store_wide(spec1, rows, forward(pairs, table, cos_ref, sin_ref))

    fill_phases(3, got_row(0))
    mix_two((2, 3), stacked(own1, got_left(0)), spec1)

    relay(0)
    direct(2)

    for t, total in enumerate((total0, total1)):
        for k in range(MIXES):
            rows = block(k)
            pairs = inverse(merged_rows(total, rows), table, cos_ref, sin_ref, gains[1:2, :])
            store_wide(spec2.at[t], rows, forward(pairs, table, cos_ref, sin_ref))

    par_copy(1).wait()
    own_copy(1).wait()
    par_copy(2).wait()
    own_copy(2).wait()
    fill_phases(5, got_row(3))
    fill_phases(6, got_row(1))
    fill_phases(7, got_row(4))
    note_owners()

    for t in range(2):
        lefts = stacked(own2, got_left(3)) if t == 0 else stacked(got_left(1), got_left(4))
        mix_two((4 + 2 * t, 5 + 2 * t), lefts, spec2.at[t])
        for slot, total in ((t, total0), (t + 2, total1)):
            for k in range(MIXES):
                rows = block(k)
                pairs = inverse(merged_rows(total, rows), table, cos_ref, sin_ref, gains[2:3, :])
                for group in range(GROUPS):
                    high, low = split(jnp.concatenate(pairs[group], axis=1))
                    out_high[slot, rows, lanes(group)] = high
                    out_low[slot, rows, lanes(group)] = low
            if t == 0 and slot == 2:
                relay(1)

    half = peers // 2
    mine = me // 2

    def weigh(slot, r):
        start, size = PARTS[r]
        rows = slice(start, start + size)
        for q in range(GROUPS):
            right = (out_high[slot, :, lanes(q)], out_low[slot, :, lanes(q)])
            matrix[slot, q, rows] = wide_product(split(wall[slot, q, rows]), right)

    def spans(r):
        start, size = PARTS[r]
        found = [(EDGE + start, size, 0, start)]
        if r == 0:
            found.append((0, EDGE, 1, 0))
        if r == len(PARTS) - 1:
            found.append((EDGE + TILE_ROWS, EDGE, -1, TILE_ROWS - EDGE))
        return found

    def reach(r):
        start, size = PARTS[r]
        first = 0 if r == 0 else EDGE + start
        last = TALL if r == len(PARTS) - 1 else EDGE + start + size
        return pl.ds(first, last - first)

    def gather(target, parity, r):
        for e in range(half):
            for at, size, step, start in spans(r):
                named = 2 * e + parity + step + 1
                value = None
                for slot in range(4):
                    for k in range(2):
                        spot = places[slot * 2 + k, named]
                        term = scales[slot * 2 + k, named] * matrix[slot, spot, start : start + size]
                        value = term if value is None else value + term
                target[e, at : at + size] = value

    def core_copy(r):
        return remote(
            away.at[:, reach(r)],
            core_got.at[:, reach(r)],
            core_send.at[r],
            core_recv.at[r],
            1,
        )

    def plane_copy(j, r):
        return remote(
            kept.at[mine ^ j, reach(r)],
            plane_got.at[j - 1, reach(r)],
            plane_send.at[0],
            plane_recv.at[r],
            2 * j,
        )

    def collect(r):
        gather(away, 1 - bits[0], r)
        core_copy(r).start()
        gather(kept, bits[0], r)

    def spread(r):
        core_copy(r).wait()
        for e in range(half):
            kept[e, reach(r)] = kept[e, reach(r)] + core_got[e, reach(r)]
        for j in range(1, half):
            plane_copy(j, r).start()

    def finish(r):
        came = plane_got.at[:, reach(r)]
        remote(came, came, plane_send.at[0], plane_recv.at[r], 2).wait_recv()
        value = kept[mine, reach(r)]
        for j in range(1, half):
            value = value + plane_got[j - 1, reach(r)]
        owned[reach(r)] = value

    loads[1].wait()
    for slot in range(4):
        if slot == 1:
            settle(0)
        weigh(slot, 0)
    collect(0)
    relay(2)
    spread(0)
    weigh(0, 1)
    settle(1)
    for slot in range(1, 4):
        weigh(slot, 1)
    collect(1)
    weigh(0, 2)
    settle(2)
    for slot in range(1, 4):
        weigh(slot, 2)
    collect(2)
    spread(1)
    spread(2)
    for r in range(len(PARTS)):
        finish(r)
    tile = owned

    low, high = slice(0, EDGE), slice(EDGE + TILE_ROWS, TALL)
    middle = slice(EDGE, EDGE + TILE_ROWS)
    cuts = [slice(plane * LANES, (plane + 1) * LANES) for plane in range(2)]
    for plane in range(2):
        flipped[plane] = tile[middle, cuts[plane]].T
    ends = [tile[rows, cut] for cut in cuts for rows in (low, high)]
    ends.append(jnp.zeros((LANES - 4 * EDGE, LANES), F32))
    flipped[2] = jnp.concatenate(ends, axis=0).T

    def halo_copy(side):
        edge = LANES - EDGE if side else 0
        return pltpu.make_async_remote_copy(
            src_ref=flipped.at[:, pl.ds(edge, EDGE)],
            dst_ref=col_halo.at[side],
            send_sem=halo_send.at[side],
            recv_sem=halo_recv.at[side],
            device_id=(me, column + (1 if side else -1)),
            device_id_type=MESH,
        )

    for side in range(2):

        @pl.when(edges[side][0])
        def _(side=side):
            halo_copy(side).start()

    sent()
    chosen = kernel_index[0]
    reach_all = 2 * REACH + 1

    def tap(u, v):
        return bank[chosen, reach_all * u + v]

    for plane in range(2):
        cut = cuts[plane]
        inner = jnp.concatenate([tile[high, cut], tile[middle, cut], tile[low, cut]], axis=0)
        whole = jnp.concatenate([inner, jnp.zeros_like(inner)], axis=1)
        summed = jnp.zeros((TILE_ROWS, LANES), F32)
        for v in range(reach_all):
            moved = whole if v == REACH else pltpu.roll(whole, (REACH - v) % WIDE, 1)
            shifted[v] = moved[:, :LANES]
            for u in range(reach_all):
                start = EDGE - REACH + u
                summed = summed + tap(u, v) * shifted[v, start : start + TILE_ROWS, :]
        inside[plane] = summed

    for side in range(2):

        @pl.when(edges[side][0])
        def _(side=side):
            halo_copy(side).wait_send()
            halo_copy(1 - side).wait_recv()

    lane = lax.broadcasted_iota(jnp.int32, (EDGE, LANES), 1)
    row = lax.broadcasted_iota(jnp.int32, (EDGE, LANES), 0)
    gap = jnp.zeros((LANES - 2 * EDGE, LANES), F32)
    for plane in range(2):
        at = plane * 2 * EDGE
        shares = []
        for side in range(2):
            ends = col_halo[side, 2]
            below = ends if at == 0 else pltpu.roll(ends, LANES - at, 1)
            above = pltpu.roll(ends, LANES - 2 * EDGE - at, 1)
            band = jnp.concatenate(
                [col_halo[side, plane], jnp.where(lane < LANES // 2, below, above)], axis=1
            )
            near = row < REACH if side == 0 else row >= EDGE - REACH
            moved = [
                band if u == REACH else pltpu.roll(band, (REACH - u) % WIDE, 1)
                for u in range(reach_all)
            ]
            moved = [jnp.where(near, m[:, :LANES], F32(0.0)) for m in moved]
            share = jnp.zeros((EDGE, LANES), F32)
            for step in range(REACH):
                v = 2 * REACH - step if side == 0 else step
                term = jnp.zeros((EDGE, LANES), F32)
                for u in range(reach_all):
                    term = term + tap(u, v) * moved[u]
                share = share + pltpu.roll(term, REACH + step if side == 0 else REACH - step, 0)
            keep = row >= EDGE - REACH if side == 0 else row < REACH
            shares.append(jnp.where(keep, share, F32(0.0)))
        result[plane] = inside[plane] + jnp.concatenate([shares[1], gap, shares[0]], axis=0).T


def short_tables():
    index = np.arange(LANES)
    angle = 2.0 * np.pi * (index[:, None] * index[None, :] % LANES) / LANES
    cos, sin = np.cos(angle), np.sin(angle)
    table = np.block([[cos, -sin], [sin, cos]]).astype(np.float32)
    high = table.astype(BF16)
    low = (table - high.astype(np.float32)).astype(BF16)
    spin = 2.0 * np.pi * (np.arange(GROUPS)[:, None] * index[None, :]) / RANGE_BINS
    return high, low, np.cos(spin).astype(np.float32), np.sin(spin).astype(np.float32)


def shards(peers, swaths, *args):
    (polar, taps, weights, shifts, gains, owner, block_weights, kernel_index, bank) = args
    sections = taps.shape[0]
    vmem = pl.BlockSpec(memory_space=pltpu.VMEM)
    smem = pl.BlockSpec(memory_space=pltpu.SMEM)
    anywhere = pl.BlockSpec(memory_space=pl.ANY)
    wide = pltpu.VMEM((ANGLES, GROUPS * WIDE), F32)
    tables = [jnp.asarray(t) for t in short_tables()]
    return pl.pallas_call(
        functools.partial(kernel, peers, swaths, sections),
        out_shape=jax.ShapeDtypeStruct((2, TILE_ROWS, LANES), F32),
        in_specs=[anywhere] + [vmem] * 4 + [smem, anywhere, smem, smem] + [vmem] * 4,
        out_specs=vmem,
        scratch_shapes=[
            pltpu.VMEM(polar.shape, F32),
            pltpu.VMEM((4, GROUPS, TILE_ROWS, ANGLES), F32),
            pltpu.VMEM((4, GROUPS, TILE_ROWS, WIDE), F32),
            pltpu.VMEM((8, GROUPS, 2, ANGLES, LANES), F32),
            *([wide] * 5),
            pltpu.VMEM((2, ANGLES, GROUPS * WIDE), F32),
            pltpu.VMEM((4, ANGLES, GROUPS * WIDE), BF16),
            pltpu.VMEM((4, ANGLES, GROUPS * WIDE), BF16),
            pltpu.VMEM((3, 3 * TAPS, LANES), F32),
            pltpu.VMEM((5, 3 * TAPS, LANES), F32),
            pltpu.SMEM((3, GROUPS), jnp.int32),
            pltpu.SMEM((8, peers + 2), jnp.int32),
            pltpu.SMEM((8, peers + 2), F32),
            *([pltpu.VMEM((peers // 2, TALL, WIDE), F32)] * 3),
            pltpu.VMEM((peers // 2 - 1, TALL, WIDE), F32),
            pltpu.VMEM((TALL, WIDE), F32),
            pltpu.VMEM((2, 3, EDGE, LANES), F32),
            pltpu.VMEM((3, LANES, LANES), F32),
            pltpu.VMEM((2 * REACH + 1, TILE_ROWS + 2 * EDGE, LANES), F32),
            pltpu.VMEM((2, TILE_ROWS, LANES), F32),
            pltpu.SemaphoreType.DMA((2,)),
            pltpu.SemaphoreType.DMA((1,)),
            pltpu.SemaphoreType.DMA((1,)),
            pltpu.SemaphoreType.DMA((3,)),
            pltpu.SemaphoreType.DMA((3,)),
            pltpu.SemaphoreType.DMA((3,)),
            pltpu.SemaphoreType.DMA((3,)),
            pltpu.SemaphoreType.DMA((1,)),
            pltpu.SemaphoreType.DMA((len(PARTS), 3)),
            pltpu.SemaphoreType.DMA((len(PARTS),)),
            pltpu.SemaphoreType.DMA((len(PARTS),)),
            pltpu.SemaphoreType.DMA((1,)),
            pltpu.SemaphoreType.DMA((len(PARTS),)),
            pltpu.SemaphoreType.DMA((2,)),
            pltpu.SemaphoreType.DMA((2,)),
        ],
        compiler_params=pltpu.CompilerParams(
            collective_id=0, has_side_effects=True, vmem_limit_bytes=60 * 2**20
        ),
    )(
        polar,
        taps,
        weights,
        shifts,
        gains,
        owner.reshape(-1),
        block_weights,
        kernel_index.reshape(-1),
        bank,
        *tables,
    )


def solution(mesh):
    peers, swaths = mesh.shape["aper"], mesh.shape["swath"]
    in_specs = (
        P(None, "aper", "swath"),
        P(None, "aper", None, None, None),
        P(None, "aper", None, None, None),
        P(None, "aper", None, None),
        P(None, "swath"),
        P("aper", "swath", None, None),
        P("aper", "swath", None, None, None),
        P("aper", "swath"),
        P(),
    )
    return jax.shard_map(
        functools.partial(shards, peers, swaths),
        mesh=mesh,
        in_specs=in_specs,
        out_specs=P(None, "aper", "swath"),
        check_vma=False,
    )
```

```python
import functools
import math

import jax
import jax.numpy as jnp
import numpy as np
from jax import lax
from jax.experimental import pallas as pl
from jax.experimental.pallas import tpu as pltpu
from jax.sharding import PartitionSpec as P

ANGLES = 128
RANGE_BINS = 1024
LANES = 128
GROUPS = RANGE_BINS // LANES
WIDE = 2 * LANES
TILE_ROWS = 128
TAPS = 8
MIXES = 4
BLOCK = ANGLES // MIXES
EDGE = 8
PARTS = ((0, 64), (64, 40), (104, 24))
TALL = TILE_ROWS + 2 * EDGE
REACH = 4
MESH = pl.DeviceIdType.MESH
F32 = jnp.float32
BF16 = jnp.bfloat16


def split(value):
    high = value.astype(BF16)
    return high, (value - high.astype(F32)).astype(BF16)


def product(left, right):
    def dot(a, b):
        return jnp.dot(a, b, preferred_element_type=F32)

    return dot(left[0], right[0]) + dot(left[1], right[0]) + dot(left[0], right[1])


def turn(value):
    half = (value - jnp.floor(value + 0.5)) * F32(math.pi)
    square = half * half
    sine = F32(-1.0 / math.factorial(15))
    for order in (13, 11, 9, 7, 5, 3, 1):
        sign = 1.0 if order % 4 == 1 else -1.0
        sine = sine * square + F32(sign / math.factorial(order))
    sine = sine * half
    cosine = F32(1.0 / math.factorial(16))
    for order in (14, 12, 10, 8, 6, 4, 2, 0):
        sign = 1.0 if order % 4 == 0 else -1.0
        cosine = cosine * square + F32(sign / math.factorial(order))
    return 1.0 - 2.0 * sine * sine, 2.0 * sine * cosine


def four(x):
    (ar, ai), (br, bi), (cr, ci), (dr, di) = x
    sr, si, tr, ti = ar + cr, ai + ci, ar - cr, ai - ci
    ur, ui, vr, vi = br + dr, bi + di, br - dr, bi - di
    return [(sr + ur, si + ui), (tr + vi, ti - vr), (sr - ur, si - ui), (tr - vi, ti + vr)]


def eight(x):
    even, odd = four(x[0::2]), four(x[1::2])
    root = F32(math.sqrt(0.5))
    turned = [
        odd[0],
        ((odd[1][0] + odd[1][1]) * root, (odd[1][1] - odd[1][0]) * root),
        (odd[2][1], -odd[2][0]),
        ((odd[3][1] - odd[3][0]) * root, -(odd[3][0] + odd[3][1]) * root),
    ]
    first = [(e[0] + o[0], e[1] + o[1]) for e, o in zip(even, turned)]
    return first + [(e[0] - o[0], e[1] - o[1]) for e, o in zip(even, turned)]


def twiddle(pairs, cos_ref, sin_ref):
    out = [pairs[0]]
    for group in range(1, GROUPS):
        a, b = pairs[group]
        c, s = cos_ref[group : group + 1, :], sin_ref[group : group + 1, :]
        out.append((a * c + b * s, b * c - a * s))
    return out


def short_dft(pairs, table):
    rows = pairs[0][0].shape[0]
    stacked = jnp.concatenate([jnp.concatenate(pair, axis=1) for pair in pairs], axis=0)
    out = product(split(stacked), table)
    return [out[g * rows : (g + 1) * rows] for g in range(len(pairs))]


def forward(pairs, table, cos_ref, sin_ref):
    return short_dft(twiddle(eight(pairs), cos_ref, sin_ref), table)


def inverse(merged, table, cos_ref, sin_ref, gain):
    out = short_dft([(im, re) for re, im in merged], table)
    pairs = eight(twiddle([(o[:, :LANES], o[:, LANES:]) for o in out], cos_ref, sin_ref))
    scaled = gain * F32(1.0 / RANGE_BINS)
    result = []
    for group, (im, re) in enumerate(pairs):
        weight = scaled[:, group * LANES : (group + 1) * LANES]
        result.append((re * weight, im * weight))
    return result


def wide_product(left, right):
    def dot(a, b):
        return jnp.dot(a, b, preferred_element_type=F32)

    both = jnp.concatenate([left[0], left[1]], axis=1)
    twice = jnp.concatenate([right[0], right[0]], axis=0)
    return dot(both, twice) + dot(left[0], right[1])


def kernel(
    peers,
    swaths,
    sections,
    polar_in,
    taps,
    weights,
    shifts,
    gains,
    owner,
    weights_in,
    kernel_index,
    bank,
    table_high,
    table_low,
    cos_ref,
    sin_ref,
    result,
    polar,
    wall,
    matrix,
    phases,
    spec0,
    got0,
    total0,
    total1,
    spec1,
    spec2,
    out_high,
    out_low,
    params,
    params_got,
    owner_got,
    places,
    scales,
    away,
    kept,
    core_got,
    plane_got,
    owned,
    col_halo,
    flipped,
    shifted,
    inside,
    in_sem,
    send_sem,
    recv_sem,
    par_send,
    par_recv,
    own_send,
    own_recv,
    w_send,
    w_recv,
    core_send,
    core_recv,
    plane_send,
    plane_recv,
    halo_send,
    halo_recv,
):
    me = lax.axis_index("aper")
    column = lax.axis_index("swath")
    levels = peers.bit_length() - 1

    col_halo[...] = jnp.zeros_like(col_halo)

    barrier = pltpu.get_barrier_semaphore()
    for level in range(levels):
        pl.semaphore_signal(
            barrier, inc=1, device_id=(me ^ (1 << level), column), device_id_type=MESH
        )
    edges = [(column > 0, column - 1), (column < swaths - 1, column + 1)]
    for within, place in edges:

        @pl.when(within)
        def _(place=place):
            pl.semaphore_signal(barrier, inc=1, device_id=(me, place), device_id_type=MESH)

    greeted = levels + sum(jnp.where(within, 1, 0) for within, _ in edges)

    loads = [
        pltpu.make_async_copy(polar_in, polar, in_sem.at[0]),
        pltpu.make_async_copy(weights_in.at[0, 0], wall.at[0], in_sem.at[1]),
    ]
    for load in loads:
        load.start()

    bits = [lax.rem(me // (1 << step), 2) for step in range(levels)]
    table = (table_high[...], table_low[...])

    def build(index, weight):
        rows = lax.broadcasted_iota(jnp.int32, (ANGLES, ANGLES), 0).astype(F32)
        built = jnp.zeros((ANGLES, ANGLES), F32)
        for tap in range(TAPS):
            built = built + jnp.where(
                index[tap : tap + 1, :] == rows, weight[tap : tap + 1, :], F32(0.0)
            )
        return built.T

    def fill_phases(place, row):
        shift = jnp.broadcast_to(row, (ANGLES, LANES)).T
        lane = lax.broadcasted_iota(jnp.int32, (ANGLES, LANES), 1)
        signed = jnp.where(lane < LANES // 2, lane, lane - LANES).astype(F32)
        unit = shift * F32(-1.0 / RANGE_BINS)
        step_cos, step_sin = turn(unit)
        a, b = turn(unit * (signed * F32(GROUPS)))
        for group in range(GROUPS):
            phases[place, group, 0] = a
            phases[place, group, 1] = b
            if group + 1 < GROUPS:
                a, b = a * step_cos - b * step_sin, b * step_cos + a * step_sin

    def own_left(step, child):
        return build(taps[step, 0, child].astype(F32), weights[step, 0, child])

    def got_left(place):
        return build(params_got[place, :TAPS], params_got[place, TAPS : 2 * TAPS])

    def own_row(step, child):
        return shifts[step, 0, pl.ds(child, 1), :]

    def got_row(place):
        return params_got[place, 2 * TAPS : 2 * TAPS + 1]

    def steered(place, group, value):
        a = phases[place, group, 0]
        b = phases[place, group, 1]
        re, im = value[:, :LANES], value[:, LANES:]
        return jnp.concatenate([a * re - b * im, b * re + a * im], axis=1)

    def lanes(group):
        return slice(group * WIDE, (group + 1) * WIDE)

    def block(k):
        return slice(k * BLOCK, (k + 1) * BLOCK)

    def store_wide(target, rows, values):
        for group in range(GROUPS):
            target[rows, lanes(group)] = values[group]

    def merged_rows(total, rows):
        pairs = []
        for group in range(GROUPS):
            value = total[rows, lanes(group)]
            pairs.append((value[:, :LANES], value[:, LANES:]))
        return pairs

    def remote(source, target, send, recv, mask):
        return pltpu.make_async_remote_copy(
            src_ref=source,
            dst_ref=target,
            send_sem=send,
            recv_sem=recv,
            device_id=(me ^ mask, column),
            device_id_type=MESH,
        )

    for place, (step, child) in enumerate(((1, 1 - bits[1]), (2, bits[2]), (2, 1 - bits[2]))):
        params[place, :TAPS] = taps[step, 0, child].astype(F32)
        params[place, TAPS : 2 * TAPS] = weights[step, 0, child]
        params[place, 2 * TAPS : 3 * TAPS] = jnp.broadcast_to(own_row(step, child), (TAPS, LANES))

    lefts0 = [split(own_left(0, child)) for child in (bits[0], 1 - bits[0])]
    fill_phases(0, own_row(0, bits[0]))
    fill_phases(1, own_row(0, 1 - bits[0]))

    def par_copy(slot):
        source, target, mask = (
            (params, params_got.at[pl.ds(0, 3)], 2),
            (params.at[2], params_got.at[3], 4),
            (params_got.at[2], params_got.at[4], 4),
        )[slot]
        return remote(source, target, par_send.at[slot], par_recv.at[slot], mask)

    def own_copy(slot):
        source, target, mask = (
            (owner, owner_got.at[0], 2),
            (owner, owner_got.at[1], 4),
            (owner_got.at[0], owner_got.at[2], 4),
        )[slot]
        return remote(source, target, own_send.at[slot], own_recv.at[slot], mask)

    def w_copy(slot, r, h):
        mask = (2, 4, 4 if h == 0 else 2)[slot]
        start, size = PARTS[r]
        piece = (pl.ds(h * (GROUPS // 2), GROUPS // 2), pl.ds(start, size))
        source = weights_in.at[0, 0] if slot < 2 else wall.at[1 if h == 0 else 2]
        return remote(
            source.at[piece],
            wall.at[slot + 1].at[piece],
            w_send.at[0],
            w_recv.at[r, h if slot == h else 2],
            mask,
        )

    def direct(r):
        for h in range(2):
            w_copy(0, r, h).start()
            w_copy(1, r, 1 - h).start()

    def relay(r):
        for h in range(2):
            w_copy(h, r, h).wait_recv()
            w_copy(2, r, h).start()

    def settle(r):
        rest = wall.at[pl.ds(1, 2), slice(None), pl.ds(*PARTS[r])]
        remote(rest, rest, w_send.at[0], w_recv.at[r, 2], 2).wait_recv()

    def sent():
        every = wall.at[pl.ds(1, 3)]
        remote(every, every, w_send.at[0], w_recv.at[0, 2], 2).wait_send()
        remote(plane_got, plane_got, plane_send.at[0], plane_recv.at[0], 2).wait_send()

    swap = remote(spec0, got0, send_sem.at[0], recv_sem.at[0], 1)

    loads[0].wait()
    for k in range(MIXES):
        rows = block(k)
        pairs = [
            (polar[0, rows, g * LANES : (g + 1) * LANES], polar[1, rows, g * LANES : (g + 1) * LANES])
            for g in range(GROUPS)
        ]
        store_wide(spec0, rows, forward(pairs, table, cos_ref, sin_ref))

    pl.semaphore_wait(barrier, greeted)
    swap.start()
    for slot in range(2):
        par_copy(slot).start()
    for slot in range(2):
        own_copy(slot).start()
    direct(0)

    def note_owners():
        for slot in range(4):
            for named in range(-1, peers + 1):
                first = jnp.int32(GROUPS)
                second = jnp.int32(GROUPS)
                for q in reversed(range(GROUPS)):
                    hit = (owner[q] if slot == 0 else owner_got[slot - 1, q]) == named
                    second = jnp.where(hit, first, second)
                    first = jnp.where(hit, q, first)
                for k, found in enumerate((first, second)):
                    places[slot * 2 + k, named + 1] = jnp.minimum(found, GROUPS - 1)
                    scales[slot * 2 + k, named + 1] = jnp.where(found < GROUPS, F32(1.0), F32(0.0))

    def mix(place, left, source, total, first):
        for group in range(GROUPS):
            value = wide_product(left, split(source[:, lanes(group)]))
            value = steered(place, group, value)
            if not first:
                value = value + total[:, lanes(group)]
            total[:, lanes(group)] = value

    def mix_two(places, left, source):
        for group in range(GROUPS):
            value = wide_product(left, split(source[:, lanes(group)]))
            for place, total, rows in zip(
                places, (total0, total1), (slice(0, ANGLES), slice(ANGLES, 2 * ANGLES))
            ):
                total[:, lanes(group)] = steered(place, group, value[rows])

    def stacked(one, two):
        return split(jnp.concatenate([one, two], axis=0))

    mix(0, lefts0[0], spec0, total0, True)
    own1 = own_left(1, bits[1])
    own2 = own_left(2, bits[2])
    fill_phases(2, own_row(1, bits[1]))
    fill_phases(4, own_row(2, bits[2]))
    swap.wait()
    par_copy(0).wait()
    own_copy(0).wait()
    par_copy(2).start()
    own_copy(2).start()
    direct(1)
    mix(1, lefts0[1], got0, total0, False)
    for k in range(MIXES):
        rows = block(k)
        pairs = inverse(merged_rows(total0, rows), table, cos_ref, sin_ref, gains[0:1, :])
        store_wide(spec1, rows, forward(pairs, table, cos_ref, sin_ref))

    fill_phases(3, got_row(0))
    mix_two((2, 3), stacked(own1, got_left(0)), spec1)

    relay(0)
    direct(2)

    for t, total in enumerate((total0, total1)):
        for k in range(MIXES):
            rows = block(k)
            pairs = inverse(merged_rows(total, rows), table, cos_ref, sin_ref, gains[1:2, :])
            store_wide(spec2.at[t], rows, forward(pairs, table, cos_ref, sin_ref))

    par_copy(1).wait()
    own_copy(1).wait()
    par_copy(2).wait()
    own_copy(2).wait()
    fill_phases(5, got_row(3))
    fill_phases(6, got_row(1))
    fill_phases(7, got_row(4))
    note_owners()

    for t in range(2):
        lefts = stacked(own2, got_left(3)) if t == 0 else stacked(got_left(1), got_left(4))
        mix_two((4 + 2 * t, 5 + 2 * t), lefts, spec2.at[t])
        for slot, total in ((t, total0), (t + 2, total1)):
            for k in range(MIXES):
                rows = block(k)
                pairs = inverse(merged_rows(total, rows), table, cos_ref, sin_ref, gains[2:3, :])
                for group in range(GROUPS):
                    high, low = split(jnp.concatenate(pairs[group], axis=1))
                    out_high[slot, rows, lanes(group)] = high
                    out_low[slot, rows, lanes(group)] = low
            if t == 0 and slot == 2:
                relay(1)

    half = peers // 2
    mine = me // 2

    def weigh(slot, r):
        start, size = PARTS[r]
        rows = slice(start, start + size)
        for q in range(GROUPS):
            right = (out_high[slot, :, lanes(q)], out_low[slot, :, lanes(q)])
            matrix[slot, q, rows] = wide_product(split(wall[slot, q, rows]), right)

    def spans(r):
        start, size = PARTS[r]
        found = [(EDGE + start, size, 0, start)]
        if r == 0:
            found.append((0, EDGE, 1, 0))
        if r == len(PARTS) - 1:
            found.append((EDGE + TILE_ROWS, EDGE, -1, TILE_ROWS - EDGE))
        return found

    def reach(r):
        start, size = PARTS[r]
        first = 0 if r == 0 else EDGE + start
        last = TALL if r == len(PARTS) - 1 else EDGE + start + size
        return pl.ds(first, last - first)

    def gather(target, parity, r):
        for e in range(half):
            for at, size, step, start in spans(r):
                named = 2 * e + parity + step + 1
                value = None
                for slot in range(4):
                    for k in range(2):
                        spot = places[slot * 2 + k, named]
                        term = scales[slot * 2 + k, named] * matrix[slot, spot, start : start + size]
                        value = term if value is None else value + term
                target[e, at : at + size] = value

    def core_copy(r):
        return remote(
            away.at[:, reach(r)],
            core_got.at[:, reach(r)],
            core_send.at[r],
            core_recv.at[r],
            1,
        )

    def plane_copy(j, r):
        return remote(
            kept.at[mine ^ j, reach(r)],
            plane_got.at[j - 1, reach(r)],
            plane_send.at[0],
            plane_recv.at[r],
            2 * j,
        )

    def collect(r):
        gather(away, 1 - bits[0], r)
        core_copy(r).start()
        gather(kept, bits[0], r)

    def spread(r):
        core_copy(r).wait()
        for e in range(half):
            kept[e, reach(r)] = kept[e, reach(r)] + core_got[e, reach(r)]
        for j in range(1, half):
            plane_copy(j, r).start()

    def finish(r):
        came = plane_got.at[:, reach(r)]
        remote(came, came, plane_send.at[0], plane_recv.at[r], 2).wait_recv()
        value = kept[mine, reach(r)]
        for j in range(1, half):
            value = value + plane_got[j - 1, reach(r)]
        owned[reach(r)] = value

    loads[1].wait()
    for slot in range(4):
        if slot == 1:
            settle(0)
        weigh(slot, 0)
    collect(0)
    relay(2)
    spread(0)
    weigh(0, 1)
    settle(1)
    for slot in range(1, 4):
        weigh(slot, 1)
    collect(1)
    weigh(0, 2)
    settle(2)
    for slot in range(1, 4):
        weigh(slot, 2)
    collect(2)
    spread(1)
    spread(2)
    for r in range(len(PARTS)):
        finish(r)
    tile = owned

    low, high = slice(0, EDGE), slice(EDGE + TILE_ROWS, TALL)
    middle = slice(EDGE, EDGE + TILE_ROWS)
    cuts = [slice(plane * LANES, (plane + 1) * LANES) for plane in range(2)]
    for plane in range(2):
        flipped[plane] = tile[middle, cuts[plane]].T
    ends = [tile[rows, cut] for cut in cuts for rows in (low, high)]
    ends.append(jnp.zeros((LANES - 4 * EDGE, LANES), F32))
    flipped[2] = jnp.concatenate(ends, axis=0).T

    def halo_copy(side):
        edge = LANES - EDGE if side else 0
        return pltpu.make_async_remote_copy(
            src_ref=flipped.at[:, pl.ds(edge, EDGE)],
            dst_ref=col_halo.at[side],
            send_sem=halo_send.at[side],
            recv_sem=halo_recv.at[side],
            device_id=(me, column + (1 if side else -1)),
            device_id_type=MESH,
        )

    for side in range(2):

        @pl.when(edges[side][0])
        def _(side=side):
            halo_copy(side).start()

    sent()
    chosen = kernel_index[0]
    reach_all = 2 * REACH + 1

    def tap(u, v):
        return bank[chosen, reach_all * u + v]

    for plane in range(2):
        cut = cuts[plane]
        inner = jnp.concatenate([tile[high, cut], tile[middle, cut], tile[low, cut]], axis=0)
        whole = jnp.concatenate([inner, jnp.zeros_like(inner)], axis=1)
        summed = jnp.zeros((TILE_ROWS, LANES), F32)
        for v in range(reach_all):
            moved = whole if v == REACH else pltpu.roll(whole, (REACH - v) % WIDE, 1)
            shifted[v] = moved[:, :LANES]
            for u in range(reach_all):
                start = EDGE - REACH + u
                summed = summed + tap(u, v) * shifted[v, start : start + TILE_ROWS, :]
        inside[plane] = summed

    for side in range(2):

        @pl.when(edges[side][0])
        def _(side=side):
            halo_copy(side).wait_send()
            halo_copy(1 - side).wait_recv()

    lane = lax.broadcasted_iota(jnp.int32, (EDGE, LANES), 1)
    row = lax.broadcasted_iota(jnp.int32, (EDGE, LANES), 0)
    gap = jnp.zeros((LANES - 2 * EDGE, LANES), F32)
    for plane in range(2):
        at = plane * 2 * EDGE
        shares = []
        for side in range(2):
            ends = col_halo[side, 2]
            below = ends if at == 0 else pltpu.roll(ends, LANES - at, 1)
            above = pltpu.roll(ends, LANES - 2 * EDGE - at, 1)
            band = jnp.concatenate(
                [col_halo[side, plane], jnp.where(lane < LANES // 2, below, above)], axis=1
            )
            near = row < REACH if side == 0 else row >= EDGE - REACH
            moved = [
                band if u == REACH else pltpu.roll(band, (REACH - u) % WIDE, 1)
                for u in range(reach_all)
            ]
            moved = [jnp.where(near, m[:, :LANES], F32(0.0)) for m in moved]
            share = jnp.zeros((EDGE, LANES), F32)
            for step in range(REACH):
                v = 2 * REACH - step if side == 0 else step
                term = jnp.zeros((EDGE, LANES), F32)
                for u in range(reach_all):
                    term = term + tap(u, v) * moved[u]
                share = share + pltpu.roll(term, REACH + step if side == 0 else REACH - step, 0)
            keep = row >= EDGE - REACH if side == 0 else row < REACH
            shares.append(jnp.where(keep, share, F32(0.0)))
        result[plane] = inside[plane] + jnp.concatenate([shares[1], gap, shares[0]], axis=0).T


def short_tables():
    index = np.arange(LANES)
    angle = 2.0 * np.pi * (index[:, None] * index[None, :] % LANES) / LANES
    cos, sin = np.cos(angle), np.sin(angle)
    table = np.block([[cos, -sin], [sin, cos]]).astype(np.float32)
    high = table.astype(BF16)
    low = (table - high.astype(np.float32)).astype(BF16)
    spin = 2.0 * np.pi * (np.arange(GROUPS)[:, None] * index[None, :]) / RANGE_BINS
    return high, low, np.cos(spin).astype(np.float32), np.sin(spin).astype(np.float32)


def shards(peers, swaths, *args):
    (polar, taps, weights, shifts, gains, owner, block_weights, kernel_index, bank) = args
    sections = taps.shape[0]
    vmem = pl.BlockSpec(memory_space=pltpu.VMEM)
    smem = pl.BlockSpec(memory_space=pltpu.SMEM)
    anywhere = pl.BlockSpec(memory_space=pl.ANY)
    wide = pltpu.VMEM((ANGLES, GROUPS * WIDE), F32)
    tables = [jnp.asarray(t) for t in short_tables()]
    return pl.pallas_call(
        functools.partial(kernel, peers, swaths, sections),
        out_shape=jax.ShapeDtypeStruct((2, TILE_ROWS, LANES), F32),
        in_specs=[anywhere] + [vmem] * 4 + [smem, anywhere, smem, smem] + [vmem] * 4,
        out_specs=vmem,
        scratch_shapes=[
            pltpu.VMEM(polar.shape, F32),
            pltpu.VMEM((4, GROUPS, TILE_ROWS, ANGLES), F32),
            pltpu.VMEM((4, GROUPS, TILE_ROWS, WIDE), F32),
            pltpu.VMEM((8, GROUPS, 2, ANGLES, LANES), F32),
            *([wide] * 5),
            pltpu.VMEM((2, ANGLES, GROUPS * WIDE), F32),
            pltpu.VMEM((4, ANGLES, GROUPS * WIDE), BF16),
            pltpu.VMEM((4, ANGLES, GROUPS * WIDE), BF16),
            pltpu.VMEM((3, 3 * TAPS, LANES), F32),
            pltpu.VMEM((5, 3 * TAPS, LANES), F32),
            pltpu.SMEM((3, GROUPS), jnp.int32),
            pltpu.SMEM((8, peers + 2), jnp.int32),
            pltpu.SMEM((8, peers + 2), F32),
            *([pltpu.VMEM((peers // 2, TALL, WIDE), F32)] * 3),
            pltpu.VMEM((peers // 2 - 1, TALL, WIDE), F32),
            pltpu.VMEM((TALL, WIDE), F32),
            pltpu.VMEM((2, 3, EDGE, LANES), F32),
            pltpu.VMEM((3, LANES, LANES), F32),
            pltpu.VMEM((2 * REACH + 1, TILE_ROWS + 2 * EDGE, LANES), F32),
            pltpu.VMEM((2, TILE_ROWS, LANES), F32),
            pltpu.SemaphoreType.DMA((2,)),
            pltpu.SemaphoreType.DMA((1,)),
            pltpu.SemaphoreType.DMA((1,)),
            pltpu.SemaphoreType.DMA((3,)),
            pltpu.SemaphoreType.DMA((3,)),
            pltpu.SemaphoreType.DMA((3,)),
            pltpu.SemaphoreType.DMA((3,)),
            pltpu.SemaphoreType.DMA((1,)),
            pltpu.SemaphoreType.DMA((len(PARTS), 3)),
            pltpu.SemaphoreType.DMA((len(PARTS),)),
            pltpu.SemaphoreType.DMA((len(PARTS),)),
            pltpu.SemaphoreType.DMA((1,)),
            pltpu.SemaphoreType.DMA((len(PARTS),)),
            pltpu.SemaphoreType.DMA((2,)),
            pltpu.SemaphoreType.DMA((2,)),
        ],
        compiler_params=pltpu.CompilerParams(
            collective_id=0, has_side_effects=True, vmem_limit_bytes=60 * 2**20
        ),
    )(
        polar,
        taps,
        weights,
        shifts,
        gains,
        owner.reshape(-1),
        block_weights,
        kernel_index.reshape(-1),
        bank,
        *tables,
    )


def solution(mesh):
    peers, swaths = mesh.shape["aper"], mesh.shape["swath"]
    in_specs = (
        P(None, "aper", "swath"),
        P(None, "aper", None, None, None),
        P(None, "aper", None, None, None),
        P(None, "aper", None, None),
        P(None, "swath"),
        P("aper", "swath", None, None),
        P("aper", "swath", None, None, None),
        P("aper", "swath"),
        P(),
    )
    return jax.shard_map(
        functools.partial(shards, peers, swaths),
        mesh=mesh,
        in_specs=in_specs,
        out_specs=P(None, "aper", "swath"),
        check_vma=False,
    )
```
